32 devices in a mesh: shard: 4 (over y, x), ctx: 4 (over z), tp: 2 (over core).
Axes of the slice: x: 2, y: 2, z: 4, core: 2. Of those that a mesh axis runs over, the one named last changes fastest.
Arguments:
- inputs: bfloat16 [4, 512, 1024], P('shard', 'ctx'), may hold values from -6 to 6
- cotangent: bfloat16 [4, 512, 1024], P('shard', 'ctx'), may hold values from -6 to 6
- mixer_matrix: float32 [1024, 4, 1024], P(('shard', 'ctx', 'tp')), may hold values from -0.1875 to 0.1875
- ffn_weight: float32 [4608, 3, 1024], P(('shard', 'ctx', 'tp')), may hold values from -0.1875 to 0.1875
- conv_weight: float32 [3, 1024], replicated, may hold values from -3.5 to 3.5
- norm_gains: float32 [2, 1024], replicated, may hold values from 0.5 to 1.5
- mixer_first: float32 [1024, 4, 1024], P(('shard', 'ctx', 'tp')), as said below
- mixer_second: float32 [1024, 4, 1024], P(('shard', 'ctx', 'tp')), as said below
- ffn_first: float32 [4608, 3, 1024], P(('shard', 'ctx', 'tp')), as said below
- ffn_second: float32 [4608, 3, 1024], P(('shard', 'ctx', 'tp')), as said below
- conv_first: float32 [3, 1024], replicated, as said below
- conv_second: float32 [3, 1024], replicated, as said below
- gain_first: float32 [2, 1024], replicated, as said below
- gain_second: float32 [2, 1024], replicated, as said below
Outputs:
- output: bfloat16 [4, 512, 1024], P('shard', 'ctx')
- input_grad: float32 [4, 512, 1024], P('shard', 'ctx')
- mixer_grad: float32 [1024, 4, 1024], P(('shard', 'ctx', 'tp'))
- ffn_grad: float32 [4608, 3, 1024], P(('shard', 'ctx', 'tp'))
- conv_grad: float32 [3, 1024], replicated
- gain_grad: float32 [2, 1024], replicated
- mixer_new: float32 [1024, 4, 1024], P(('shard', 'ctx', 'tp'))
- ffn_new: float32 [4608, 3, 1024], P(('shard', 'ctx', 'tp'))
- conv_new: float32 [3, 1024], replicated
- gain_new: float32 [2, 1024], replicated
- mixer_first_new: float32 [1024, 4, 1024], P(('shard', 'ctx', 'tp'))
- mixer_second_new: float32 [1024, 4, 1024], P(('shard', 'ctx', 'tp'))
- ffn_first_new: float32 [4608, 3, 1024], P(('shard', 'ctx', 'tp'))
- ffn_second_new: float32 [4608, 3, 1024], P(('shard', 'ctx', 'tp'))
- conv_first_new: float32 [3, 1024], replicated
- conv_second_new: float32 [3, 1024], replicated
- gain_first_new: float32 [2, 1024], replicated
- gain_second_new: float32 [2, 1024], replicated
The draws below stay inside these ranges and needn't reach their ends.
Inputs may be any that keep to these rules, and one draw needn't show every extreme that they name: `mixer_first`: a running mean of earlier gradients. `mixer_second`: a running mean of squared earlier gradients. `ffn_first`: a running mean of earlier gradients. `ffn_second`: a running mean of squared earlier gradients. `conv_first`: a running mean of earlier gradients. `conv_second`: a running mean of squared earlier gradients. `gain_first`: a running mean of earlier gradients. `gain_second`: a running mean of squared earlier gradients.
All inputs are finite; a program needn't handle non-finite values.
Results may differ from the reference program's by a relative error of at most 0.009.
The reference program's roundings to bfloat16 on the way count: a program that leaves them out, or rounds other values in their place, can miss the bound.
Values may be sent and summed in bfloat16 or wider, within the bound.
No kernel may reach another device: no remote copies, remote signals or barrier semaphores. Data moves between devices by JAX's collectives and lax.ppermute only.
A program may use at most 192 MiB of HBM per device.

```python
import math
import jax
import jax.numpy as jnp
from jax import lax

D = 1024
FF = 4608
STEP = 10
SEQS = 4
LEN = 512


def first_moment(key, salt, shape):
    noise = jax.random.normal(jax.random.fold_in(key, salt), shape, jnp.float32)
    return 0.03 * math.sqrt(SEQS * LEN) * noise


def second_moment(key, salt, shape):
    noise = jax.random.normal(jax.random.fold_in(key, salt), shape, jnp.float32)
    return 9e-05 * (SEQS * LEN) * (noise * noise + 0.3)


def draw_mixer_first(key, part):
    return first_moment(key, 101, (D, 4, D))


def draw_mixer_second(key, part):
    return second_moment(key, 102, (D, 4, D))


def draw_ffn_first(key, part):
    return first_moment(key, 103, (FF, 3, D))


def draw_ffn_second(key, part):
    return second_moment(key, 104, (FF, 3, D))


def draw_conv_first(key, part):
    return first_moment(key, 105, (3, D))


def draw_conv_second(key, part):
    return second_moment(key, 106, (3, D))


def draw_gain_first(key, part):
    return first_moment(key, 107, (2, D))


def draw_gain_second(key, part):
    return second_moment(key, 108, (2, D))


def shard_levels(own_key, dims, cuts, least, top_value):
    factor_of, own = 1.0, jax.random.fold_in(own_key, 6)
    for axis_at, blocks in cuts:
        steps = jnp.exp(jax.random.uniform(jax.random.fold_in(own, axis_at), (blocks,), jnp.float32, least / len(cuts), top_value / len(cuts)))
        factor_of = factor_of * jnp.repeat(steps, dims[axis_at] // blocks).reshape([-1 if axis == axis_at else 1 for axis in range(len(dims))])
    return factor_of


def scatter_about(key, dims, spread, reach, shards=(), kind=jnp.bfloat16):
    drawn = jax.random.normal(key, dims, jnp.float32) * spread
    if len(shards) > 0:
        drawn = shard_levels(key, dims, shards, -0.22, 0.18) * drawn
    return jnp.clip(drawn, min=-reach, max=reach).astype(kind)


def setup_inputs(seed: int = 0) -> dict:
    seeds = jax.random.split(jax.random.key(seed), 15)
    return {
        "inputs": scatter_about(seeds[0], (SEQS, LEN, D), 1.0, 6.0, ((0, 4), (1, 4))),
        "cotangent": scatter_about(seeds[1], (SEQS, LEN, D), 1.0, 6.0, ((0, 4), (1, 4))),
        "mixer_matrix": scatter_about(seeds[2], (D, 4, D), D ** -0.5, 0.1875, ((0, 32),), jnp.float32),
        "ffn_weight": scatter_about(seeds[3], (FF, 3, D), D ** -0.5, 0.1875, ((0, 32),), jnp.float32),
        "conv_weight": scatter_about(seeds[4], (3, D), 3 ** -0.5, 3.5, (), jnp.float32),
        "norm_gains": jnp.clip(1.0 + 0.1 * jax.random.normal(seeds[5], (2, D), jnp.float32), 0.5, 1.5),
        "mixer_first": draw_mixer_first(jax.random.fold_in(seeds[14], 71), 0),
        "mixer_second": draw_mixer_second(jax.random.fold_in(seeds[14], 71), 0),
        "ffn_first": draw_ffn_first(jax.random.fold_in(seeds[14], 71), 0),
        "ffn_second": draw_ffn_second(jax.random.fold_in(seeds[14], 71), 0),
        "conv_first": draw_conv_first(jax.random.fold_in(seeds[14], 71), 0),
        "conv_second": draw_conv_second(jax.random.fold_in(seeds[14], 71), 0),
        "gain_first": draw_gain_first(jax.random.fold_in(seeds[14], 71), 0),
        "gain_second": draw_gain_second(jax.random.fold_in(seeds[14], 71), 0),
    }


norm_eps = 1e-05
beta_first = 0.9
beta_second = 0.999
adam_eps = 1e-08
matrix_rate = 0.02
small_rate = 0.25
decay_rate = 0.1

def rounded_value(values):
    return lax.optimization_barrier(values.astype(jnp.bfloat16)).astype(jnp.float32)

def rms_scale(values):
    return lax.rsqrt(lax.optimization_barrier(jnp.mean(values * values, axis=-1, keepdims=True)) + norm_eps)

def norm_backward(grad_normed, normed, scale):
    return scale * (grad_normed - normed * lax.optimization_barrier(jnp.mean(grad_normed * normed, axis=-1, keepdims=True)))

def adam_update(weight, gradient, first, second, rate, decay):
    first_new = beta_first * first + (1.0 - beta_first) * gradient
    second_new = beta_second * second + (1.0 - beta_second) * gradient * gradient
    first_hat = first_new / (1.0 - beta_first ** STEP)
    second_hat = second_new / (1.0 - beta_second ** STEP)
    weight_new = weight - rate * (first_hat / (jnp.sqrt(second_hat) + adam_eps) + decay * weight)
    return (weight_new, first_new, second_new)

def reference(inputs, cotangent, mixer_matrix, ffn_weight, conv_weight, norm_gains, mixer_first, mixer_second, ffn_first, ffn_second, conv_first, conv_second, gain_first, gain_second):
    w_mix = rounded_value(mixer_matrix)
    w_ffn = rounded_value(ffn_weight)
    model_width = inputs.shape[2]
    seq_len = inputs.shape[1]
    zero_pad = jnp.zeros((2, model_width), jnp.float32)

    def one_sequence(running_total, pieces):
        mix_acc, ffn_acc, tap_acc, gain_acc = running_total
        seq_in, seq_cot = pieces
        x_rows = seq_in.astype(jnp.float32)
        scale_one = rms_scale(x_rows)
        normed_one = x_rows * scale_one
        h_one = rounded_value(normed_one * norm_gains[0])
        projected = jnp.einsum('ld,ckd->lkc', h_one, w_mix[:, :3, :])
        in_b = projected[:, 0, :]
        in_c = projected[:, 1, :]
        in_x = projected[:, 2, :]
        product = in_b * in_x
        padded = jnp.concatenate([zero_pad, product], axis=0)
        mixed_rows = conv_weight[0] * padded[:seq_len] + conv_weight[1] * padded[1:seq_len + 1] + conv_weight[2] * padded[2:]
        gated = rounded_value(in_c * mixed_rows)
        mix_out = jnp.dot(gated, w_mix[:, 3, :], preferred_element_type=jnp.float32)
        residual = x_rows + mix_out
        scale_two = rms_scale(residual)
        normed_two = residual * scale_two
        h_two = rounded_value(normed_two * norm_gains[1])
        gate_and_lift = jnp.einsum('ld,ckd->lkc', h_two, w_ffn[:, :2, :])
        gate_pre = gate_and_lift[:, 0, :]
        up_value = gate_and_lift[:, 1, :]
        sigmoid_gate = jax.nn.sigmoid(gate_pre)
        gate_act = gate_pre * sigmoid_gate
        hidden = rounded_value(gate_act * up_value)
        ffn_out = jnp.dot(hidden, w_ffn[:, 2, :], preferred_element_type=jnp.float32)
        out_rows = (residual + ffn_out).astype(jnp.bfloat16)
        grad_float = seq_cot.astype(jnp.float32)
        grad_hidden = jnp.dot(grad_float, w_ffn[:, 2, :].T, preferred_element_type=jnp.float32)
        grad_gate = rounded_value(grad_hidden * up_value * sigmoid_gate * (1.0 + gate_pre * (1.0 - sigmoid_gate)))
        grad_up = rounded_value(grad_hidden * gate_act)
        grad_pair = jnp.stack([grad_gate, grad_up], axis=1)
        grad_h_two = jnp.einsum('lkc,ckd->ld', grad_pair, w_ffn[:, :2, :])
        ffn_in_term = jnp.einsum('lkc,ld->ckd', grad_pair, h_two)
        ffn_down_term = jnp.dot(hidden.T, grad_float, preferred_element_type=jnp.float32)
        ffn_term = jnp.concatenate([ffn_in_term, ffn_down_term[:, None, :]], axis=1)
        grad_resid = grad_float + norm_backward(grad_h_two * norm_gains[1], normed_two, scale_two)
        grad_mix = rounded_value(grad_resid)
        grad_gated = jnp.dot(grad_mix, w_mix[:, 3, :].T, preferred_element_type=jnp.float32)
        grad_mixed = grad_gated * in_c
        grad_c = grad_gated * mixed_rows
        grad_pad = jnp.concatenate([grad_mixed, zero_pad], axis=0)
        grad_prod = conv_weight[2] * grad_mixed + conv_weight[1] * grad_pad[1:seq_len + 1] + conv_weight[0] * grad_pad[2:]
        gradient_triple = rounded_value(jnp.stack([grad_prod * in_x, grad_c, grad_prod * in_b], axis=1))
        grad_h_one = jnp.einsum('lkc,ckd->ld', gradient_triple, w_mix[:, :3, :])
        mix_in_term = jnp.einsum('lkc,ld->ckd', gradient_triple, h_one)
        mix_out_term = jnp.dot(gated.T, grad_mix, preferred_element_type=jnp.float32)
        mixer_term = jnp.concatenate([mix_in_term, mix_out_term[:, None, :]], axis=1)
        tap_term = jnp.stack([lax.optimization_barrier(jnp.sum(grad_mixed * padded[:seq_len], axis=0)), lax.optimization_barrier(jnp.sum(grad_mixed * padded[1:seq_len + 1], axis=0)), lax.optimization_barrier(jnp.sum(grad_mixed * padded[2:], axis=0))])
        gain_term = jnp.stack([lax.optimization_barrier(jnp.sum(grad_h_one * normed_one, axis=0)), lax.optimization_barrier(jnp.sum(grad_h_two * normed_two, axis=0))])
        input_rows = grad_resid + norm_backward(grad_h_one * norm_gains[0], normed_one, scale_one)
        updated = (mix_acc + mixer_term, ffn_acc + ffn_term, tap_acc + tap_term, gain_acc + gain_term)
        return (updated, (out_rows, input_rows))
    start_sums = (jnp.zeros(w_mix.shape, jnp.float32), jnp.zeros(w_ffn.shape, jnp.float32), jnp.zeros(conv_weight.shape, jnp.float32), jnp.zeros(norm_gains.shape, jnp.float32))
    sums, outs = lax.scan(one_sequence, start_sums, (inputs, cotangent))
    mixer_grad, ffn_grad, conv_grad, gain_grad = sums
    output, input_grad = outs
    mixer_new, mixer_first_new, mixer_second_new = adam_update(mixer_matrix, mixer_grad, mixer_first, mixer_second, matrix_rate, decay_rate)
    ffn_new, ffn_first_new, ffn_second_new = adam_update(ffn_weight, ffn_grad, ffn_first, ffn_second, matrix_rate, decay_rate)
    conv_new, conv_first_new, conv_second_new = adam_update(conv_weight, conv_grad, conv_first, conv_second, small_rate, 0.0)
    gain_new, gain_first_new, gain_second_new = adam_update(norm_gains, gain_grad, gain_first, gain_second, small_rate, 0.0)
    return (output, input_grad, mixer_grad, ffn_grad, conv_grad, gain_grad, mixer_new, ffn_new, conv_new, gain_new, mixer_first_new, mixer_second_new, ffn_first_new, ffn_second_new, conv_first_new, conv_second_new, gain_first_new, gain_second_new)
```

```python
import jax
import jax.numpy as jnp
from jax import lax
from jax.sharding import PartitionSpec as P

STEP = 10


norm_eps = 1e-05
beta_first = 0.9
beta_second = 0.999
adam_eps = 1e-08
matrix_rate = 0.02
small_rate = 0.25
decay_rate = 0.1

bf16 = jnp.bfloat16
f32 = jnp.float32


def rms_scale(values):
    return lax.rsqrt(jnp.mean(values * values, axis=-1, keepdims=True) + norm_eps)


def norm_backward(grad_normed, normed, scale):
    return scale * (grad_normed - normed * jnp.mean(grad_normed * normed, axis=-1, keepdims=True))


def adam_update(weight, gradient, first, second, rate, decay):
    first_new = beta_first * first + (1.0 - beta_first) * gradient
    second_new = beta_second * second + (1.0 - beta_second) * gradient * gradient
    first_hat = first_new / (1.0 - beta_first**STEP)
    second_hat = second_new / (1.0 - beta_second**STEP)
    weight_new = weight - rate * (first_hat / (jnp.sqrt(second_hat) + adam_eps) + decay * weight)
    return (weight_new, first_new, second_new)


def partner_of(index, step, count):
    if count & (count - 1) == 0:
        return index ^ step
    return (step - index) % count


def swap_with(value, axis, step):
    count = lax.axis_size(axis)
    return lax.ppermute(
        value, axis, [(i, partner_of(i, step, count)) for i in range(count)]
    )


def send_up(value, axis, steps):
    count = lax.axis_size(axis)
    return lax.ppermute(value, axis, [(i, (i + steps) % count) for i in range(count)])


def after(value, *others):
    return lax.optimization_barrier((value, *others))[0]


def tree_sum(values):
    while len(values) > 1:
        values = [a + b for a, b in zip(values[::2], values[1::2])]
    return values[0]


def sum_over(value, axis):
    count = lax.axis_size(axis)
    if count & (count - 1):
        return lax.psum(value, axis)
    return tree_sum([value] + [swap_with(value, axis, k) for k in range(1, count)])


def spread_rows(own):
    count = lax.axis_size("ctx")
    mine = jnp.concatenate([own] + [send_up(own, "ctx", -k) for k in range(1, count)], axis=0)
    return jnp.concatenate([mine, swap_with(mine, "tp", 1)], axis=0)


def collect_rows(kept, sent):
    count = lax.axis_size("ctx")
    rows = kept.shape[0] // count
    pair = kept + swap_with(sent, "tp", 1).astype(f32)
    total = pair[:rows]
    for k in range(1, count):
        piece = pair[k * rows : (k + 1) * rows].astype(bf16)
        total = total + send_up(piece, "ctx", k).astype(f32)
    return total


def per_device(
    inputs,
    cotangent,
    mixer_matrix,
    ffn_weight,
    conv_weight,
    norm_gains,
    mixer_first,
    mixer_second,
    ffn_first,
    ffn_second,
    conv_first,
    conv_second,
    gain_first,
    gain_second,
):
    shard_count = lax.axis_size("shard")
    ctx_count = lax.axis_size("ctx")
    tp_count = lax.axis_size("tp")
    seq_count, tok_count, width = inputs.shape
    assert seq_count == 1 and tp_count == 2
    shard_at = lax.axis_index("shard")
    ctx_at = lax.axis_index("ctx")
    tp_at = lax.axis_index("tp")
    half = tok_count // tp_count
    seq_len = tok_count * ctx_count
    first_core = tp_at == 0

    def own_half(rows):
        return lax.dynamic_slice_in_dim(rows[0], tp_at * half, half, axis=0)

    def both_halves(mine):
        other = swap_with(mine, "tp", 1)
        return jnp.concatenate(
            [jnp.where(first_core, mine, other), jnp.where(first_core, other, mine)], axis=0
        )[None]

    def in_order(rows):
        mine = rows[: seq_len // 2].reshape(ctx_count, half, -1)
        other = rows[seq_len // 2 :].reshape(ctx_count, half, -1)
        low, high = jnp.where(first_core, mine, other), jnp.where(first_core, other, mine)
        return jnp.stack([low, high], axis=1).reshape(seq_len, -1)

    def out_of_order(rows):
        rows = rows.reshape(ctx_count, 2, half, -1)
        low, high = rows[:, 0], rows[:, 1]
        mine, other = jnp.where(first_core, low, high), jnp.where(first_core, high, low)
        return jnp.concatenate(
            [mine.reshape(seq_len // 2, -1), other.reshape(seq_len // 2, -1)], axis=0
        )

    mixer_own = mixer_matrix.transpose(1, 0, 2).astype(bf16)
    ffn_own = ffn_weight.transpose(1, 0, 2).astype(bf16)
    mixer_parts = [mixer_own] + [swap_with(mixer_own, "shard", k) for k in range(1, shard_count)]
    x_half = own_half(inputs)
    x_all = spread_rows(x_half)
    ffn_sent = after(ffn_own, *mixer_parts)
    ffn_parts = [ffn_own] + [swap_with(ffn_sent, "shard", k) for k in range(1, shard_count)]
    g_half = own_half(cotangent)
    g_all = spread_rows(after(g_half, x_all))

    mixer_w = jnp.concatenate(mixer_parts, axis=1)
    ffn_w = jnp.concatenate(ffn_parts, axis=1)
    channels, hidden = mixer_w.shape[1], ffn_w.shape[1]

    block = channels // shard_count
    grouped_at = partner_of(jnp.arange(shard_count), shard_at, shard_count)
    tap_grid = conv_weight.reshape(3, shard_count, ctx_count * tp_count, block)
    tap_grid = lax.dynamic_index_in_dim(tap_grid, ctx_at * tp_count + tp_at, 2, keepdims=False)
    taps = jnp.take(tap_grid, grouped_at, axis=1).reshape(3, channels)

    gain_one, gain_two = norm_gains[0], norm_gains[1]

    def by_rows(rows, weight):
        return lax.dot_general(
            rows, weight, (((1,), (1,)), ((), ())), preferred_element_type=f32
        )

    def down_rows(left, right):
        return lax.dot_general(
            left, right, (((0,), (0,)), ((), ())), preferred_element_type=f32
        )

    x_float = x_all.astype(f32)
    scale_one = rms_scale(x_float)
    normed_one = x_float * scale_one
    h_one = (normed_one * gain_one).astype(bf16)
    in_b = by_rows(h_one, mixer_w[0])
    in_c = by_rows(h_one, mixer_w[1])
    in_x = by_rows(h_one, mixer_w[2])
    position = (jnp.arange(seq_len) + ctx_at * tok_count) % seq_len
    position = position[:, None]

    def earlier(rows, steps):
        return jnp.where(position >= steps, jnp.roll(rows, steps, axis=0), 0.0)

    def later(rows, steps):
        return jnp.where(position < seq_len - steps, jnp.roll(rows, -steps, axis=0), 0.0)

    product = in_order(in_b * in_x)
    product_one, product_two = earlier(product, 1), earlier(product, 2)
    mixed = out_of_order(taps[0] * product_two + taps[1] * product_one + taps[2] * product)
    gated = (in_c * mixed).astype(bf16)
    part = jnp.dot(gated, mixer_w[3], preferred_element_type=f32)
    mine_count = seq_len // 2
    mix_out = collect_rows(part[:mine_count], part[mine_count:].astype(bf16))

    x_own = x_half.astype(f32)
    residual = x_own + mix_out
    scale_two = rms_scale(residual)
    normed_two = residual * scale_two
    h_two = spread_rows((normed_two * gain_two).astype(bf16))

    gate_pre = by_rows(h_two, ffn_w[0])
    up_value = by_rows(h_two, ffn_w[1])
    sigmoid_gate = jax.nn.sigmoid(gate_pre)
    gate_act = gate_pre * sigmoid_gate
    act = (gate_act * up_value).astype(bf16)
    grad_act = by_rows(g_all, ffn_w[2])
    grad_gate = (
        grad_act * up_value * sigmoid_gate * (1.0 + gate_pre * (1.0 - sigmoid_gate))
    ).astype(bf16)
    grad_up = (grad_act * gate_act).astype(bf16)
    part = jnp.dot(grad_gate, ffn_w[0], preferred_element_type=f32) + jnp.dot(
        grad_up, ffn_w[1], preferred_element_type=f32
    )
    grad_h_two = collect_rows(part[:mine_count], part[mine_count:].astype(bf16))
    g_own = g_half.astype(f32)
    grad_resid = g_own + norm_backward(grad_h_two * gain_two, normed_two, scale_two)
    grad_mix_own = grad_resid.astype(bf16)
    grad_mix = spread_rows(grad_mix_own)

    part = jnp.dot(act, ffn_w[2], preferred_element_type=f32)
    ffn_out = collect_rows(part[:mine_count], part[mine_count:].astype(bf16))
    output = both_halves((residual + ffn_out).astype(bf16))

    def owners_sum(grads, rows):
        total = grads[:, :rows]
        for k in range(1, shard_count):
            piece = grads[:, k * rows : (k + 1) * rows].astype(bf16)
            total = total + swap_with(piece, "shard", k).astype(f32)
        return total

    ffn_terms = jnp.stack(
        [down_rows(grad_gate, h_two), down_rows(grad_up, h_two), down_rows(act, g_all)]
    )
    ffn_grad = owners_sum(ffn_terms, hidden // shard_count).transpose(1, 0, 2)

    grad_gated = by_rows(grad_mix, mixer_w[3])
    grad_c = grad_gated * mixed
    grad_mixed = in_order(grad_gated * in_c)
    grad_prod = out_of_order(
        taps[0] * later(grad_mixed, 2) + taps[1] * later(grad_mixed, 1) + taps[2] * grad_mixed
    )
    tap_grads = jnp.stack(
        [
            jnp.sum(grad_mixed * product_two, axis=0),
            jnp.sum(grad_mixed * product_one, axis=0),
            jnp.sum(grad_mixed * product, axis=0),
        ]
    )
    grad_b = (grad_prod * in_x).astype(bf16)
    grad_c = grad_c.astype(bf16)
    grad_x = (grad_prod * in_b).astype(bf16)
    part = (
        jnp.dot(grad_b, mixer_w[0], preferred_element_type=f32)
        + jnp.dot(grad_c, mixer_w[1], preferred_element_type=f32)
        + jnp.dot(grad_x, mixer_w[2], preferred_element_type=f32)
    )
    grad_h_one = collect_rows(part[:mine_count], part[mine_count:].astype(bf16))
    gain_part = jnp.sum(part * normed_one, axis=0)
    mixer_terms = jnp.stack(
        [
            down_rows(grad_b, h_one),
            down_rows(grad_c, h_one),
            down_rows(grad_x, h_one),
            down_rows(gated, grad_mix),
        ]
    )
    mixer_grad = owners_sum(mixer_terms, block).transpose(1, 0, 2)

    spread = jnp.take(tap_grads.reshape(3, shard_count, block), grouped_at, axis=1)
    blank = jnp.zeros((3, shard_count, ctx_count * tp_count, block), f32)
    spread = lax.dynamic_update_index_in_dim(blank, spread, ctx_at * tp_count + tp_at, 2)
    small = jnp.concatenate(
        [
            gain_part[None],
            jnp.sum(grad_h_two * normed_two, axis=0)[None],
            spread.reshape(3, width),
        ],
        axis=0,
    )
    small = sum_over(sum_over(sum_over(small, "tp"), "shard"), "ctx")
    gain_grad, conv_grad = small[:2], small[2:]

    x_scale = rms_scale(x_own)
    x_normed = x_own * x_scale
    input_grad = both_halves(
        grad_resid + norm_backward(grad_h_one * gain_one, x_normed, x_scale)
    )

    mixer_new, mixer_first_new, mixer_second_new = adam_update(
        mixer_matrix, mixer_grad, mixer_first, mixer_second, matrix_rate, decay_rate
    )
    ffn_new, ffn_first_new, ffn_second_new = adam_update(
        ffn_weight, ffn_grad, ffn_first, ffn_second, matrix_rate, decay_rate
    )
    conv_new, conv_first_new, conv_second_new = adam_update(
        conv_weight, conv_grad, conv_first, conv_second, small_rate, 0.0
    )
    gain_new, gain_first_new, gain_second_new = adam_update(
        norm_gains, gain_grad, gain_first, gain_second, small_rate, 0.0
    )
    return (
        output,
        input_grad,
        mixer_grad,
        ffn_grad,
        conv_grad,
        gain_grad,
        mixer_new,
        ffn_new,
        conv_new,
        gain_new,
        mixer_first_new,
        mixer_second_new,
        ffn_first_new,
        ffn_second_new,
        conv_first_new,
        conv_second_new,
        gain_first_new,
        gain_second_new,
    )


def solution(mesh):
    tokens = P("shard", "ctx", None)
    rows = P(("shard", "ctx", "tp"), None, None)
    in_specs = (tokens, tokens, rows, rows, P(), P(), rows, rows, rows, rows, P(), P(), P(), P())
    out_specs = (
        (tokens, tokens, rows, rows, P(), P(), rows, rows, P(), P())
        + (rows, rows, rows, rows)
        + (P(), P(), P(), P())
    )
    return jax.shard_map(
        per_device, mesh=mesh, in_specs=in_specs, out_specs=out_specs, check_vma=False
    )
```

```python
import functools

import jax
import jax.numpy as jnp
from jax import lax
from jax.experimental import pallas as pl
from jax.experimental.pallas import tpu as pltpu
from jax.sharding import PartitionSpec as P


STEP = 10


norm_eps = 1e-05
beta_first = 0.9
beta_second = 0.999
adam_eps = 1e-08
matrix_rate = 0.02
small_rate = 0.25
decay_rate = 0.1

bf16 = jnp.bfloat16
f32 = jnp.float32


def norm_backward(grad_normed, normed, scale):
    return scale * (grad_normed - normed * jnp.mean(grad_normed * normed, axis=-1, keepdims=True))


def adam_update(weight, gradient, first, second, rate, decay):
    first_new = beta_first * first + (1.0 - beta_first) * gradient
    second_new = beta_second * second + (1.0 - beta_second) * gradient * gradient
    first_hat = first_new / (1.0 - beta_first**STEP)
    second_hat = second_new / (1.0 - beta_second**STEP)
    weight_new = weight - rate * (first_hat / (jnp.sqrt(second_hat) + adam_eps) + decay * weight)
    return (weight_new, first_new, second_new)


def partner_of(index, step, count):
    assert count & (count - 1) == 0
    return index ^ step


def swap_with(value, axis, step):
    count = lax.axis_size(axis)
    return lax.ppermute(
        value, axis, [(i, partner_of(i, step, count)) for i in range(count)]
    )


def send_up(value, axis, steps):
    count = lax.axis_size(axis)
    return lax.ppermute(value, axis, [(i, (i + steps) % count) for i in range(count)])


def tree_sum(values):
    while len(values) > 1:
        values = [a + b for a, b in zip(values[::2], values[1::2])]
    return values[0]


def sum_over(value, axis):
    count = lax.axis_size(axis)
    return tree_sum([value] + [swap_with(value, axis, k) for k in range(1, count)])


def spread_rows(own):
    count = lax.axis_size("ctx")
    mine = [own] + [send_up(own, "ctx", -k) for k in range(1, count)]
    return mine + [swap_with(piece, "tp", 1) for piece in mine]


def in_vmem(body, outs, *operands, scalars=None, scratch=(), flops=0):
    specs = [pl.BlockSpec(memory_space=pltpu.VMEM)] * len(operands)
    if scalars is not None:
        specs = [pl.BlockSpec(memory_space=pltpu.SMEM)] + specs
        operands = (scalars, *operands)
    shapes = [jax.ShapeDtypeStruct(shape, dtype) for shape, dtype in outs]
    moved = sum(x.size * x.dtype.itemsize for x in (*operands, *shapes))
    return pl.pallas_call(
        body,
        out_shape=shapes,
        in_specs=specs,
        out_specs=[pl.BlockSpec(memory_space=pltpu.VMEM)] * len(shapes),
        scratch_shapes=list(scratch),
        compiler_params=pltpu.CompilerParams(vmem_limit_bytes=48 << 20),
        cost_estimate=pl.CostEstimate(flops=flops, bytes_accessed=moved, transcendentals=0),
    )(*operands)


def by_rows(rows, weight):
    return lax.dot_general(rows, weight, (((1,), (1,)), ((), ())), preferred_element_type=f32)


def down_rows(left, right):
    return lax.dot_general(left, right, (((0,), (0,)), ((), ())), preferred_element_type=f32)


def block_start(piece, core, rows):
    return pl.multiple_of((2 * piece + core) * rows, rows)


def masked_roll(values, steps, length, zero_rows):
    rolled = pltpu.roll(values, steps % length, 0)
    row = lax.broadcasted_iota(jnp.int32, values.shape, 0)
    kept = row != zero_rows[0]
    for at in zero_rows[1:]:
        kept = kept & (row != at)
    return jnp.where(kept, rolled, 0.0)


def convolved(b_part, x_part, taps, length, first):
    product = b_part * x_part
    second = lax.rem(first + 1, length)
    one = masked_roll(product, 1, length, (first,))
    two = masked_roll(product, 2, length, (first, second))
    return product, one, two, taps[0:1] * two + taps[1:2] * one + taps[2:3] * product


def own_columns(groups, block, at_ref, shape):
    row = lax.broadcasted_iota(jnp.int32, shape, 0)
    ahead = lax.broadcasted_iota(jnp.int32, shape, 1) - row
    stride = shape[1] // groups
    found = jnp.zeros(shape, f32)
    for k in range(groups):
        base = jnp.bitwise_xor(at_ref[2], k) * stride + (at_ref[3] - k) * block
        inside = (row >= k * block) & (row < (k + 1) * block)
        found = jnp.where(inside & (ahead == base), 1.0, found)
    return found


def mixer_forward(count, groups, at_ref, *refs):
    pieces, parts = refs[: 2 * count], refs[2 * count : 2 * count + groups]
    gain_ref, conv_ref, h_ref, w_ref, p_ref, y_ref, taps_ref, keep_ref, send_ref = refs[
        2 * count + groups :
    ]
    rows, length = pieces[0].shape[0], h_ref.shape[0]
    block, channels = parts[0].shape[1], y_ref.shape[1]
    core, first = at_ref[0], at_ref[1]
    taps_ref[...] = lax.dot_general(
        conv_ref[...],
        own_columns(groups, block, at_ref, (channels, conv_ref.shape[1])),
        (((1,), (1,)), ((), ())),
        precision=lax.Precision.HIGHEST,
        preferred_element_type=f32,
    )
    for k in range(4):
        for s in range(groups):
            w_ref[k * channels + s * block : k * channels + (s + 1) * block, :] = parts[s][k]
    gain = gain_ref[...]
    for j in range(2 * count):
        x = pieces[j][...].astype(f32)
        scale = lax.rsqrt(jnp.mean(x * x, axis=-1, keepdims=True) + norm_eps)
        side = core if j < count else 1 - core
        h_ref[pl.ds(block_start(j % count, side, rows), rows), :] = (x * scale * gain).astype(bf16)
    p_ref[...] = by_rows(h_ref[...], w_ref[: 3 * channels, :])
    in_b, in_c = p_ref[:, :channels], p_ref[:, channels : 2 * channels]
    in_x = p_ref[:, 2 * channels :]
    mixed = convolved(in_b, in_x, taps_ref[...], length, first)[3]
    y_ref[...] = (in_c * mixed).astype(bf16)
    out_w = w_ref[3 * channels :, :]
    for side, out_ref in ((1 - core, send_ref), (core, keep_ref)):
        rows_of = [y_ref[pl.ds(block_start(k, side, rows), rows), :] for k in range(count)]
        part = jnp.dot(jnp.concatenate(rows_of, axis=0), out_w, preferred_element_type=f32)
        out_ref[...] = part.astype(out_ref.dtype)


def mixer_backward(count, groups, at_ref, *refs):
    pieces = refs[: 2 * count]
    h_ref, w_ref, p_ref, gain_ref, taps_ref, gain_two_ref = refs[2 * count : 2 * count + 6]
    dm_ref, dp_ref, small_ref, keep_ref, send_ref = refs[2 * count + 6 :]
    rows, length = pieces[0].shape[0], h_ref.shape[0]
    channels = taps_ref.shape[1]
    core, first = at_ref[0], at_ref[1]
    for j in range(2 * count):
        side = core if j < count else 1 - core
        dm_ref[pl.ds(block_start(j % count, side, rows), rows), :] = pieces[j][...]
    grad_gated = by_rows(dm_ref[...], w_ref[3 * channels :, :])
    in_b, in_c = p_ref[:, :channels], p_ref[:, channels : 2 * channels]
    in_x = p_ref[:, 2 * channels :]
    taps = taps_ref[...]
    product, one, two, mixed = convolved(in_b, in_x, taps, length, first)
    grad_mixed = grad_gated * in_c
    last = lax.rem(first + length - 1, length)
    before = lax.rem(first + length - 2, length)
    next_one = masked_roll(grad_mixed, -1, length, (last,))
    next_two = masked_roll(grad_mixed, -2, length, (last, before))
    grad_prod = taps[0:1] * next_two + taps[1:2] * next_one + taps[2:3] * grad_mixed
    dp_ref[:, :channels] = (grad_prod * in_x).astype(bf16)
    dp_ref[:, channels : 2 * channels] = (grad_gated * mixed).astype(bf16)
    dp_ref[:, 2 * channels :] = (grad_prod * in_b).astype(bf16)
    tap_sums = [
        jnp.sum(grad_mixed * shifted, axis=0, keepdims=True) for shifted in (two, one, product)
    ]
    small_ref[2:, :] = jnp.dot(
        jnp.concatenate(tap_sums, axis=0),
        own_columns(groups, channels // groups, at_ref, (channels, h_ref.shape[1])),
        precision=lax.Precision.HIGHEST,
        preferred_element_type=f32,
    )
    small_ref[1:2, :] = gain_two_ref[...]
    gain_sum = jnp.zeros(gain_ref.shape, f32)
    for side, out_ref in ((1 - core, send_ref), (core, keep_ref)):
        starts = [block_start(k, side, rows) for k in range(count)]
        grads = jnp.concatenate([dp_ref[pl.ds(at, rows), :] for at in starts], axis=0)
        part = jnp.dot(grads, w_ref[: 3 * channels, :], preferred_element_type=f32)
        out_ref[...] = part.astype(out_ref.dtype)
        normed = jnp.concatenate([h_ref[pl.ds(at, rows), :] for at in starts], axis=0)
        gain_sum = gain_sum + jnp.sum(part * normed.astype(f32), axis=0, keepdims=True)
    small_ref[0:1, :] = gain_sum / gain_ref[...]


def mixer_weight_grads(groups, dp_ref, h_ref, y_ref, dm_ref, *outs):
    block = outs[0].shape[1]
    channels = y_ref.shape[1]
    inner = down_rows(dp_ref[...], h_ref[...])
    outer = down_rows(y_ref[...], dm_ref[...])
    for s in range(groups):
        for k in range(3):
            at = k * channels + s * block
            outs[s][k] = inner[at : at + block].astype(outs[s].dtype)
        outs[s][3] = outer[s * block : (s + 1) * block].astype(outs[s].dtype)


def ffn_rows(count, groups, *refs):
    pieces, g_pieces = refs[: 2 * count], refs[2 * count : 4 * count]
    parts = refs[4 * count : 4 * count + groups]
    h_ref, g_ref, act_ref, gate_ref, up_ref, down_ref, keep_ref, send_ref, w_ref = refs[
        4 * count + groups :
    ]
    rows, block, hidden = pieces[0].shape[0], parts[0].shape[1], down_ref.shape[0]
    for j in range(2 * count):
        h_ref[j * rows : (j + 1) * rows, :] = pieces[j][...]
        g_ref[j * rows : (j + 1) * rows, :] = g_pieces[j][...]
    for s in range(groups):
        for k in range(2):
            at = k * hidden + s * block
            w_ref[at : at + block, :] = parts[s][k]
        down_ref[s * block : (s + 1) * block, :] = parts[s][2]
    side_rows = count * rows
    for at, out_ref in ((side_rows, send_ref), (0, keep_ref)):
        these = slice(at, at + side_rows)
        gate = by_rows(h_ref[these, :], w_ref[:hidden, :])
        up = by_rows(h_ref[these, :], w_ref[hidden:, :])
        sigmoid = jax.nn.sigmoid(gate)
        gate_act = gate * sigmoid
        act_ref[these, :] = (gate_act * up).astype(bf16)
        grad_act = by_rows(g_ref[these, :], down_ref[...])
        up_ref[these, :] = (grad_act * gate_act).astype(bf16)
        gate_ref[these, :] = (
            grad_act * up * sigmoid * (1.0 + gate * (1.0 - sigmoid))
        ).astype(bf16)
        part = jnp.dot(gate_ref[these, :], w_ref[:hidden, :], preferred_element_type=f32)
        part = part + jnp.dot(up_ref[these, :], w_ref[hidden:, :], preferred_element_type=f32)
        out_ref[...] = part.astype(out_ref.dtype)


def ffn_down(act_ref, down_ref, keep_ref, send_ref):
    half = keep_ref.shape[0]
    for at, out_ref in ((half, send_ref), (0, keep_ref)):
        part = jnp.dot(act_ref[at : at + half, :], down_ref[...], preferred_element_type=f32)
        out_ref[...] = part.astype(out_ref.dtype)


def ffn_weight_grads(groups, gate_ref, up_ref, act_ref, h_ref, g_ref, *outs):
    block = outs[0].shape[1]
    for k, (left, right) in enumerate(((gate_ref, h_ref), (up_ref, h_ref), (act_ref, g_ref))):
        term = down_rows(left[...], right[...])
        for s in range(groups):
            outs[s][k] = term[s * block : (s + 1) * block].astype(outs[s].dtype)


def mixer_adam(groups, *refs):
    own_ref, *parts = refs[:groups]
    weight, first, second, grad_out, weight_out, first_out, second_out = refs[groups:]
    for k in range(4):
        grad = own_ref[k]
        for part in parts:
            grad = grad + part[k].astype(f32)
        news = adam_update(
            weight[:, k, :], grad, first[:, k, :], second[:, k, :], matrix_rate, decay_rate
        )
        grad_out[:, k, :] = grad
        for out, new in zip((weight_out, first_out, second_out), news):
            out[:, k, :] = new


def pair_kernel(kept_ref, got_ref, *outs):
    rows = outs[0].shape[0]
    for k, out_ref in enumerate(outs):
        at = slice(k * rows, (k + 1) * rows)
        out_ref[...] = (kept_ref[at, :] + got_ref[at, :].astype(f32)).astype(out_ref.dtype)


def total_of(own_ref, got_refs):
    total = own_ref[...]
    for got in got_refs:
        total = total + got[...].astype(f32)
    return total


def second_norm(*refs):
    own_ref, *got = refs[:-5]
    x_ref, gain_ref, resid_ref, normed_ref, h_ref = refs[-5:]
    residual = x_ref[...].astype(f32) + total_of(own_ref, got)
    resid_ref[...] = residual
    normed = residual * lax.rsqrt(jnp.mean(residual * residual, axis=-1, keepdims=True) + norm_eps)
    normed_ref[...] = normed
    h_ref[...] = (normed * gain_ref[...]).astype(bf16)


def second_norm_backward(*refs):
    own_ref, *got = refs[:-7]
    resid_ref, normed_ref, g_ref, gain_ref, grad_ref, dm_ref, gain_part_ref = refs[-7:]
    grad_h = total_of(own_ref, got)
    normed, residual = normed_ref[...], resid_ref[...]
    scale = lax.rsqrt(jnp.mean(residual * residual, axis=-1, keepdims=True) + norm_eps)
    grad = g_ref[...].astype(f32) + norm_backward(grad_h * gain_ref[...], normed, scale)
    grad_ref[...] = grad
    dm_ref[...] = grad.astype(bf16)
    gain_part_ref[...] = jnp.sum(grad_h * normed, axis=0, keepdims=True)


def first_norm_backward(*refs):
    own_ref, *got = refs[:-4]
    x_ref, grad_ref, gain_ref, out_ref = refs[-4:]
    x = x_ref[...].astype(f32)
    scale = lax.rsqrt(jnp.mean(x * x, axis=-1, keepdims=True) + norm_eps)
    out_ref[...] = grad_ref[...] + norm_backward(
        total_of(own_ref, got) * gain_ref[...], x * scale, scale
    )


def output_kernel(*refs):
    own_ref, *got = refs[:-2]
    resid_ref, out_ref = refs[-2:]
    out_ref[...] = (resid_ref[...] + total_of(own_ref, got)).astype(out_ref.dtype)


def collect_rows(kept, sent):
    count = lax.axis_size("ctx")
    rows, width = kept.shape[0] // count, kept.shape[1]
    outs = [((rows, width), f32)] + [((rows, width), bf16)] * (count - 1)
    got = swap_with(sent, "tp", 1)
    pieces = in_vmem(pair_kernel, outs, kept, got)
    return [pieces[0]] + [send_up(pieces[k], "ctx", k) for k in range(1, count)]


def per_device(
    inputs,
    cotangent,
    mixer_matrix,
    ffn_weight,
    conv_weight,
    norm_gains,
    mixer_first,
    mixer_second,
    ffn_first,
    ffn_second,
    conv_first,
    conv_second,
    gain_first,
    gain_second,
):
    shard_count = lax.axis_size("shard")
    ctx_count = lax.axis_size("ctx")
    tp_count = lax.axis_size("tp")
    seq_count, tok_count, width = inputs.shape
    assert seq_count == 1 and tp_count == 2
    shard_at = lax.axis_index("shard")
    ctx_at = lax.axis_index("ctx")
    tp_at = lax.axis_index("tp")
    half = tok_count // tp_count
    seq_len = tok_count * ctx_count
    first_core = tp_at == 0

    def own_half(rows):
        return lax.dynamic_slice_in_dim(rows[0], tp_at * half, half, axis=0)

    def both_halves(mine):
        other = swap_with(mine, "tp", 1)
        return jnp.concatenate(
            [jnp.where(first_core, mine, other), jnp.where(first_core, other, mine)], axis=0
        )[None]

    x_half = own_half(inputs)
    x_pieces = spread_rows(x_half)
    mixer_own = mixer_matrix.transpose(1, 0, 2).astype(bf16)
    mixer_parts = [mixer_own] + [swap_with(mixer_own, "shard", k) for k in range(1, shard_count)]
    g_half = own_half(cotangent)
    g_pieces = spread_rows(g_half)
    ffn_own = ffn_weight.transpose(1, 0, 2).astype(bf16)
    ffn_parts = [ffn_own] + [swap_with(ffn_own, "shard", k) for k in range(1, shard_count)]

    block, ffn_block = mixer_own.shape[1], ffn_own.shape[1]
    channels, hidden = block * shard_count, ffn_block * shard_count
    first = (seq_len - ctx_at * tok_count) % seq_len
    scalars = jnp.stack([tp_at, first, shard_at, ctx_at * tp_count + tp_at]).astype(jnp.int32)
    gain_one, gain_two = norm_gains[0:1], norm_gains[1:2]
    mine_count = seq_len // 2
    half_shape, half_sent = ((half, width), f32), ((half, width), bf16)
    parted = [((mine_count, width), f32), ((mine_count, width), bf16)]

    h_one, mixer_w, projected, gated, taps, kept, sent = in_vmem(
        functools.partial(mixer_forward, ctx_count, shard_count),
        [
            ((seq_len, width), bf16),
            ((4 * channels, width), bf16),
            ((seq_len, 3 * channels), f32),
            ((seq_len, channels), bf16),
            ((3, channels), f32),
        ]
        + parted,
        *x_pieces,
        *mixer_parts,
        gain_one,
        conv_weight,
        scalars=scalars,
        flops=8 * seq_len * channels * width,
    )
    residual, normed_two, h_two_own = in_vmem(
        second_norm,
        [half_shape, half_shape, half_sent],
        *collect_rows(kept, sent),
        x_half,
        gain_two,
    )

    hidden_rows = ((seq_len, hidden), bf16)
    h_two, g_all, act, grad_gate, grad_up, down_w, kept, sent = in_vmem(
        functools.partial(ffn_rows, ctx_count, shard_count),
        [
            ((seq_len, width), bf16),
            ((seq_len, width), bf16),
            hidden_rows,
            hidden_rows,
            hidden_rows,
            ((hidden, width), bf16),
        ]
        + parted,
        *spread_rows(h_two_own),
        *g_pieces,
        *ffn_parts,
        scratch=[pltpu.VMEM((2 * hidden, width), bf16)],
        flops=10 * seq_len * hidden * width,
    )
    grad_resid, grad_mix_own, gain_two_part = in_vmem(
        second_norm_backward,
        [half_shape, half_sent, ((1, width), f32)],
        *collect_rows(kept, sent),
        residual,
        normed_two,
        g_half,
        gain_two,
    )
    kept, sent = in_vmem(ffn_down, parted, act, down_w, flops=2 * seq_len * hidden * width)
    ffn_pieces = collect_rows(kept, sent)
    ffn_terms = in_vmem(
        functools.partial(ffn_weight_grads, shard_count),
        [((3, ffn_block, width), f32)] + [((3, ffn_block, width), bf16)] * (shard_count - 1),
        grad_gate,
        grad_up,
        act,
        h_two,
        g_all,
        flops=6 * seq_len * hidden * width,
    )
    ffn_got = [swap_with(ffn_terms[k], "shard", k) for k in range(1, shard_count)]

    grad_mix_all, grad_triple, small, kept, sent = in_vmem(
        functools.partial(mixer_backward, ctx_count, shard_count),
        [
            ((seq_len, width), bf16),
            ((seq_len, 3 * channels), bf16),
            ((5, width), f32),
        ]
        + parted,
        *spread_rows(grad_mix_own),
        h_one,
        mixer_w,
        projected,
        gain_one,
        taps,
        gain_two_part,
        scalars=scalars,
        flops=8 * seq_len * channels * width,
    )
    in_pieces = collect_rows(kept, sent)
    mixer_terms = in_vmem(
        functools.partial(mixer_weight_grads, shard_count),
        [((4, block, width), f32)] + [((4, block, width), bf16)] * (shard_count - 1),
        grad_triple,
        h_one,
        gated,
        grad_mix_all,
        flops=8 * seq_len * channels * width,
    )
    mixer_got = [swap_with(mixer_terms[k], "shard", k) for k in range(1, shard_count)]
    small = sum_over(sum_over(small, "tp"), "shard")
    small = sum_over(small, "ctx")
    gain_grad, conv_grad = small[:2], small[2:]

    ffn_grad = ffn_terms[0]
    for got in ffn_got:
        ffn_grad = ffn_grad + got.astype(f32)
    ffn_grad = ffn_grad.transpose(1, 0, 2)
    ffn_new, ffn_first_new, ffn_second_new = adam_update(
        ffn_weight, ffn_grad, ffn_first, ffn_second, matrix_rate, decay_rate
    )
    out_own = in_vmem(output_kernel, [half_sent], *ffn_pieces, residual)[0]
    output = both_halves(out_own)
    input_grad = both_halves(
        in_vmem(first_norm_backward, [half_shape], *in_pieces, x_half, grad_resid, gain_one)[0],
    )
    mixer_grad, mixer_new, mixer_first_new, mixer_second_new = in_vmem(
        functools.partial(mixer_adam, shard_count),
        [(mixer_matrix.shape, f32)] * 4,
        mixer_terms[0],
        *mixer_got,
        mixer_matrix,
        mixer_first,
        mixer_second,
    )
    conv_new, conv_first_new, conv_second_new = adam_update(
        conv_weight, conv_grad, conv_first, conv_second, small_rate, 0.0
    )
    gain_new, gain_first_new, gain_second_new = adam_update(
        norm_gains, gain_grad, gain_first, gain_second, small_rate, 0.0
    )
    return (
        output,
        input_grad,
        mixer_grad,
        ffn_grad,
        conv_grad,
        gain_grad,
        mixer_new,
        ffn_new,
        conv_new,
        gain_new,
        mixer_first_new,
        mixer_second_new,
        ffn_first_new,
        ffn_second_new,
        conv_first_new,
        conv_second_new,
        gain_first_new,
        gain_second_new,
    )


def solution(mesh):
    tokens = P("shard", "ctx", None)
    rows = P(("shard", "ctx", "tp"), None, None)
    in_specs = (tokens, tokens, rows, rows, P(), P(), rows, rows, rows, rows, P(), P(), P(), P())
    out_specs = (
        (tokens, tokens, rows, rows, P(), P(), rows, rows, P(), P())
        + (rows, rows, rows, rows)
        + (P(), P(), P(), P())
    )

    return jax.shard_map(
        per_device, mesh=mesh, in_specs=in_specs, out_specs=out_specs, check_vma=False
    )
```

```python
import functools

import jax
import jax.numpy as jnp
from jax import lax
from jax.experimental import pallas as pl
from jax.experimental.pallas import tpu as pltpu
from jax.sharding import PartitionSpec as P


STEP = 10


norm_eps = 1e-05
beta_first = 0.9
beta_second = 0.999
adam_eps = 1e-08
matrix_rate = 0.02
small_rate = 0.25
decay_rate = 0.1
small_rows = 8

bf16 = jnp.bfloat16
f32 = jnp.float32


def norm_backward(grad_normed, normed, scale):
    return scale * (grad_normed - normed * jnp.mean(grad_normed * normed, axis=-1, keepdims=True))


def adam_update(weight, gradient, first, second, rate, decay):
    first_new = beta_first * first + (1.0 - beta_first) * gradient
    second_new = beta_second * second + (1.0 - beta_second) * gradient * gradient
    first_hat = first_new / (1.0 - beta_first**STEP)
    second_hat = second_new / (1.0 - beta_second**STEP)
    weight_new = weight - rate * (first_hat / (jnp.sqrt(second_hat) + adam_eps) + decay * weight)
    return (weight_new, first_new, second_new)


def partner_of(index, step, count):
    assert count & (count - 1) == 0
    return index ^ step


def swap_with(value, axis, step):
    count = lax.axis_size(axis)
    return lax.ppermute(
        value, axis, [(i, partner_of(i, step, count)) for i in range(count)]
    )


def tree_sum(values):
    while len(values) > 1:
        values = [a + b for a, b in zip(values[::2], values[1::2])]
    return values[0]


def across_shard(halves):
    count = lax.axis_size("shard")
    pieces = [list(halves)]
    for k in range(1, count):
        low, high = k & -k, 1 << (k.bit_length() - 1)
        pieces.append(
            [swap_with(pieces[k ^ via][j], "shard", via) for j, via in enumerate((low, high))]
        )
    return pieces


def spread_rows(own):
    count = lax.axis_size("ctx")
    mine = [own]
    for k in range(1, count):
        if k == 1 or k % 2 == 0:
            mine.append(swap_with(own, "ctx", k))
        else:
            mine.append(swap_with(mine[k - 1], "ctx", 1))
    return mine + [swap_with(piece, "tp", 1) for piece in mine]


def in_vmem(body, outs, *operands, scratch=(), flops=0, mib=16):
    shapes = [jax.ShapeDtypeStruct(shape, dtype) for shape, dtype in outs]
    moved = sum(x.size * x.dtype.itemsize for x in (*operands, *shapes))
    return pl.pallas_call(
        body,
        out_shape=shapes,
        in_specs=[pl.BlockSpec(memory_space=pltpu.VMEM)] * len(operands),
        out_specs=[pl.BlockSpec(memory_space=pltpu.VMEM)] * len(shapes),
        scratch_shapes=list(scratch),
        compiler_params=pltpu.CompilerParams(vmem_limit_bytes=mib << 20),
        cost_estimate=pl.CostEstimate(flops=flops, bytes_accessed=moved, transcendentals=0),
    )(*operands)


def by_rows(rows, weight):
    return lax.dot_general(rows, weight, (((1,), (1,)), ((), ())), preferred_element_type=f32)


def down_rows(left, right):
    return lax.dot_general(left, right, (((0,), (0,)), ((), ())), preferred_element_type=f32)


def block_start(step, core, rows):
    return pl.multiple_of((2 * jnp.bitwise_xor(lax.axis_index("ctx"), step) + core) * rows, rows)


def delayed(values, steps):
    length = values.shape[0]
    rolled = pltpu.roll(values, steps % length, 0)
    row = lax.broadcasted_iota(jnp.int32, values.shape, 0)
    kept = row >= steps if steps > 0 else row < length + steps
    return jnp.where(kept, rolled, 0.0)


def convolved(b_part, x_part, taps):
    product = b_part * x_part
    one, two = delayed(product, 1), delayed(product, 2)
    return product, one, two, taps[0:1] * two + taps[1:2] * one + taps[2:3] * product


def own_columns(groups, block, shape):
    row = lax.broadcasted_iota(jnp.int32, shape, 0)
    ahead = lax.broadcasted_iota(jnp.int32, shape, 1) - row
    stride = shape[1] // groups
    found = jnp.zeros(shape, f32)
    group_at = lax.axis_index("shard")
    within = lax.axis_index("ctx") * lax.axis_size("tp") + lax.axis_index("tp")
    for k in range(groups):
        base = jnp.bitwise_xor(group_at, k) * stride + (within - k) * block
        inside = (row >= k * block) & (row < (k + 1) * block)
        found = jnp.where(inside & (ahead == base), 1.0, found)
    return found


def mixer_forward(count, groups, *refs):
    pieces, parts = refs[: 2 * count], refs[2 * count : 2 * count + groups]
    gain_ref, conv_ref, h_ref, w_ref, p_ref, y_ref, taps_ref, keep_ref, send_ref = refs[
        2 * count + groups :
    ]
    rows = pieces[0].shape[0]
    block, channels = parts[0].shape[1], y_ref.shape[1]
    core = lax.axis_index("tp")
    taps_ref[...] = lax.dot_general(
        conv_ref[...],
        own_columns(groups, block, (channels, conv_ref.shape[1])),
        (((1,), (1,)), ((), ())),
        precision=lax.Precision.HIGHEST,
        preferred_element_type=f32,
    )
    for k in range(4):
        for s in range(groups):
            w_ref[k * channels + s * block : k * channels + (s + 1) * block, :] = parts[s][k]
    gain = gain_ref[0:1, :]
    for j in range(2 * count):
        x = pieces[j][...].astype(f32)
        scale = lax.rsqrt(jnp.mean(x * x, axis=-1, keepdims=True) + norm_eps)
        side = core if j < count else 1 - core
        h_ref[pl.ds(block_start(j % count, side, rows), rows), :] = (x * scale * gain).astype(bf16)
    p_ref[...] = by_rows(h_ref[...], w_ref[: 3 * channels, :])
    in_b, in_c = p_ref[:, :channels], p_ref[:, channels : 2 * channels]
    in_x = p_ref[:, 2 * channels :]
    mixed = convolved(in_b, in_x, taps_ref[...])[3]
    y_ref[...] = (in_c * mixed).astype(bf16)
    out_w = w_ref[3 * channels :, :]
    for side, out_ref in ((1 - core, send_ref), (core, keep_ref)):
        starts = [block_start(k, side, rows) for k in range(count)]
        rows_of = [y_ref[pl.ds(at, rows), :] for at in starts]
        part = jnp.dot(jnp.concatenate(rows_of, axis=0), out_w, preferred_element_type=f32)
        out_ref[...] = part.astype(out_ref.dtype)


def halves_of(values):
    coarse = values.astype(bf16)
    return coarse, (values - coarse.astype(f32)).astype(bf16)


def whole_of(ref, at):
    rows = small_rows
    return ref[at : at + rows, :].astype(f32) + ref[at + rows : at + 2 * rows, :].astype(f32)


def mixer_backward(count, groups, *refs):
    pieces = refs[: 2 * count]
    h_ref, w_ref, p_ref, gain_ref, taps_ref, gain_two_ref = refs[2 * count : 2 * count + 6]
    dm_ref, dp_ref, keep_ref, send_ref, small_ref = refs[2 * count + 6 :]
    rows, side_rows = pieces[0].shape[0], count * pieces[0].shape[0]
    channels = taps_ref.shape[1]
    core = lax.axis_index("tp")
    for j in range(2 * count):
        side = core if j < count else 1 - core
        dm_ref[pl.ds(block_start(j % count, side, rows), rows), :] = pieces[j][...]
    grad_gated = by_rows(dm_ref[...], w_ref[3 * channels :, :])
    in_b, in_c = p_ref[:, :channels], p_ref[:, channels : 2 * channels]
    in_x = p_ref[:, 2 * channels :]
    taps = taps_ref[...]
    product, one, two, mixed = convolved(in_b, in_x, taps)
    grad_mixed = grad_gated * in_c
    next_one, next_two = delayed(grad_mixed, -1), delayed(grad_mixed, -2)
    grad_prod = taps[0:1] * next_two + taps[1:2] * next_one + taps[2:3] * grad_mixed
    dp_ref[:, :channels] = (grad_prod * in_x).astype(bf16)
    dp_ref[:, channels : 2 * channels] = (grad_gated * mixed).astype(bf16)
    dp_ref[:, 2 * channels :] = (grad_prod * in_b).astype(bf16)
    tap_sums = [
        jnp.sum(grad_mixed * shifted, axis=0, keepdims=True) for shifted in (two, one, product)
    ]
    small_ref[...] = jnp.zeros(small_ref.shape, f32)
    small_ref[2:5, :] = jnp.dot(
        jnp.concatenate(tap_sums, axis=0),
        own_columns(groups, channels // groups, (channels, h_ref.shape[1])),
        precision=lax.Precision.HIGHEST,
        preferred_element_type=f32,
    )
    small_ref[1:2, :] = gain_two_ref[...]
    gain_sum = jnp.zeros((1, gain_ref.shape[1]), f32)
    for side, out_ref in ((1 - core, send_ref), (core, keep_ref)):
        starts = [block_start(k, side, rows) for k in range(count)]
        grads = jnp.concatenate([dp_ref[pl.ds(at, rows), :] for at in starts], axis=0)
        part = jnp.dot(grads, w_ref[: 3 * channels, :], preferred_element_type=f32)
        out_ref[:side_rows, :] = part.astype(out_ref.dtype)
        normed = jnp.concatenate([h_ref[pl.ds(at, rows), :] for at in starts], axis=0)
        gain_sum = gain_sum + jnp.sum(part * normed.astype(f32), axis=0, keepdims=True)
    small_ref[0:1, :] = gain_sum / gain_ref[0:1, :]
    coarse, fine = halves_of(small_ref[...])
    send_ref[side_rows:, :] = jnp.concatenate([coarse, fine], axis=0)
    keep_ref[side_rows:, :] = coarse.astype(f32) + fine.astype(f32)


def mixer_weight_grads(groups, dp_ref, h_ref, y_ref, dm_ref, *outs):
    block = outs[0].shape[1]
    channels = y_ref.shape[1]
    inner = down_rows(dp_ref[...], h_ref[...])
    outer = down_rows(y_ref[...], dm_ref[...])
    for s in range(groups):
        for k in range(3):
            at = k * channels + s * block
            outs[s][k] = inner[at : at + block].astype(outs[s].dtype)
        outs[s][3] = outer[s * block : (s + 1) * block].astype(outs[s].dtype)


def ffn_gather(count, *refs):
    *pieces, g_ref, w_ref, down_ref = refs
    g_pieces, parts = pieces[: 2 * count], pieces[2 * count :]
    rows, hidden = g_pieces[0].shape[0], down_ref.shape[0]
    for j in range(2 * count):
        g_ref[j * rows : (j + 1) * rows, :] = g_pieces[j][...]
    block, columns = parts[0].shape[1:]
    for j, part in enumerate(parts):
        at, side = (j // 2) * block, slice((j % 2) * columns, (j % 2 + 1) * columns)
        w_ref[at : at + block, side] = part[0]
        w_ref[hidden + at : hidden + at + block, side] = part[1]
        down_ref[at : at + block, side] = part[2]


def ffn_rows(count, *refs):
    pieces = refs[: 2 * count]
    g_ref, w_ref, down_ref, h_ref, act_ref, gate_ref, up_ref, keep_ref, send_ref = refs[2 * count :]
    rows, hidden = pieces[0].shape[0], down_ref.shape[0]
    for j in range(2 * count):
        h_ref[j * rows : (j + 1) * rows, :] = pieces[j][...]
    side_rows = count * rows
    for at, out_ref in ((side_rows, send_ref), (0, keep_ref)):
        these = slice(at, at + side_rows)
        gate = by_rows(h_ref[these, :], w_ref[:hidden, :])
        up = by_rows(h_ref[these, :], w_ref[hidden:, :])
        sigmoid = jax.nn.sigmoid(gate)
        gate_act = gate * sigmoid
        act_ref[these, :] = (gate_act * up).astype(bf16)
        grad_act = by_rows(g_ref[these, :], down_ref[...])
        up_ref[these, :] = (grad_act * gate_act).astype(bf16)
        gate_ref[these, :] = (
            grad_act * up * sigmoid * (1.0 + gate * (1.0 - sigmoid))
        ).astype(bf16)
        part = jnp.dot(gate_ref[these, :], w_ref[:hidden, :], preferred_element_type=f32)
        part = part + jnp.dot(up_ref[these, :], w_ref[hidden:, :], preferred_element_type=f32)
        out_ref[...] = part.astype(out_ref.dtype)


def ffn_down(act_ref, down_ref, keep_ref, send_ref):
    half = keep_ref.shape[0]
    for at, out_ref in ((half, send_ref), (0, keep_ref)):
        part = jnp.dot(act_ref[at : at + half, :], down_ref[...], preferred_element_type=f32)
        out_ref[...] = part.astype(out_ref.dtype)


def ffn_weight_grads(groups, gate_ref, up_ref, act_ref, h_ref, g_ref, *outs):
    block = outs[0].shape[1]
    for k, (left, right) in enumerate(((gate_ref, h_ref), (up_ref, h_ref), (act_ref, g_ref))):
        term = down_rows(left[...], right[...])
        for s in range(groups):
            outs[s][k] = term[s * block : (s + 1) * block].astype(outs[s].dtype)


def ffn_adam(groups, *refs):
    own_ref, *parts = refs[:groups]
    weight, first, second, grad_out, *outs = refs[groups:]
    for k in range(3):
        grad = own_ref[k]
        for part in parts:
            grad = grad + part[k].astype(f32)
        grad_out[k] = grad
        news = adam_update(weight[k], grad, first[k], second[k], matrix_rate, decay_rate)
        for out, new in zip(outs, news):
            out[k] = new


def mixer_adam(groups, *refs):
    own_ref, *parts = refs[:groups]
    weight, first, second, grad_out, weight_out, first_out, second_out = refs[groups:]
    for k in range(4):
        grad = own_ref[k]
        for part in parts:
            grad = grad + part[k].astype(f32)
        news = adam_update(
            weight[:, k, :], grad, first[:, k, :], second[:, k, :], matrix_rate, decay_rate
        )
        grad_out[:, k, :] = grad
        for out, new in zip((weight_out, first_out, second_out), news):
            out[:, k, :] = new


def pair_kernel(kept_ref, got_ref, *outs):
    rows = outs[0].shape[0]
    for k, out_ref in enumerate(outs):
        at = slice(k * rows, (k + 1) * rows)
        out_ref[...] = (kept_ref[at, :] + got_ref[at, :].astype(f32)).astype(out_ref.dtype)


def pair_with_small(kept_ref, got_ref, *outs):
    rows = outs[0].shape[0] - small_rows
    count = len(outs)
    small = kept_ref[count * rows :, :] + whole_of(got_ref, count * rows)
    coarse, fine = halves_of(small)
    for k, out_ref in enumerate(outs):
        at = slice(k * rows, (k + 1) * rows)
        pair = kept_ref[at, :] + got_ref[at, :].astype(f32)
        out_ref[:rows, :] = pair.astype(out_ref.dtype)
        if k == 0:
            out_ref[rows:, :] = coarse.astype(f32) + fine.astype(f32)
        else:
            out_ref[rows:, :] = jnp.concatenate([coarse, fine], axis=0)


def total_of(own_ref, got_refs, rows=None):
    total = own_ref[:rows, :]
    for got in got_refs:
        total = total + got[:rows, :].astype(f32)
    return total


def own_rows(rows_ref, out_ref):
    count = out_ref.shape[0]
    start = pl.multiple_of(lax.axis_index("tp") * count, count)
    out_ref[...] = rows_ref[0, pl.ds(start, count), :]


def join_rows(mine_ref, other_ref, out_ref):
    count, core = mine_ref.shape[0], lax.axis_index("tp")
    out_ref[0, pl.ds(pl.multiple_of(core * count, count), count), :] = mine_ref[...]
    out_ref[0, pl.ds(pl.multiple_of((1 - core) * count, count), count), :] = other_ref[...]


def prepare_ffn(weight_ref, *outs):
    columns = outs[0].shape[2]
    for j, out_ref in enumerate(outs):
        out_ref[...] = weight_ref[:, :, j * columns : (j + 1) * columns].astype(bf16)


def prepare_mixer(weight_ref, out_ref):
    for k in range(4):
        out_ref[k] = weight_ref[:, k, :].astype(bf16)


def second_norm(*refs):
    own_ref, *got = refs[:-5]
    x_ref, gain_ref, resid_ref, normed_ref, h_ref = refs[-5:]
    residual = x_ref[...].astype(f32) + total_of(own_ref, got)
    resid_ref[...] = residual
    normed = residual * lax.rsqrt(jnp.mean(residual * residual, axis=-1, keepdims=True) + norm_eps)
    normed_ref[...] = normed
    h_ref[...] = (normed * gain_ref[1:2, :]).astype(bf16)


def second_norm_backward(*refs):
    own_ref, *got = refs[:-7]
    resid_ref, normed_ref, g_ref, gain_ref, grad_ref, dm_ref, gain_part_ref = refs[-7:]
    grad_h = total_of(own_ref, got)
    normed, residual = normed_ref[...], resid_ref[...]
    scale = lax.rsqrt(jnp.mean(residual * residual, axis=-1, keepdims=True) + norm_eps)
    grad = g_ref[...].astype(f32) + norm_backward(grad_h * gain_ref[1:2, :], normed, scale)
    grad_ref[...] = grad
    dm_ref[...] = grad.astype(bf16)
    gain_part_ref[...] = jnp.sum(grad_h * normed, axis=0, keepdims=True)


def first_norm_backward(*refs):
    own_ref, *got = refs[:-5]
    x_ref, grad_ref, gain_ref, out_ref, small_ref = refs[-5:]
    rows = x_ref.shape[0]
    x = x_ref[...].astype(f32)
    scale = lax.rsqrt(jnp.mean(x * x, axis=-1, keepdims=True) + norm_eps)
    out_ref[...] = grad_ref[...] + norm_backward(
        total_of(own_ref, got, rows) * gain_ref[0:1, :], x * scale, scale
    )
    small_ref[...] = tree_sum([own_ref[rows:, :]] + [whole_of(ref, rows) for ref in got])


def small_adam(groups, *refs):
    pieces, operands, outs = refs[:groups], refs[groups : groups + 6], refs[groups + 6 :]
    total = tree_sum([piece[...] for piece in pieces])
    for which, grad in enumerate((total[0:2], total[2:5])):
        weight, first, second = (ref[...] for ref in operands[3 * which : 3 * which + 3])
        news = adam_update(weight, grad, first, second, small_rate, 0.0)
        for out, value in zip(outs[4 * which : 4 * which + 4], (grad, *news)):
            out[...] = value


def output_kernel(*refs):
    own_ref, *got = refs[:-2]
    resid_ref, out_ref = refs[-2:]
    out_ref[...] = (resid_ref[...] + total_of(own_ref, got)).astype(out_ref.dtype)


def collect_rows(kept, sent, small=False):
    count = lax.axis_size("ctx")
    width = kept.shape[1]
    rows = (kept.shape[0] - small_rows * small) // count
    outs = [((rows + small_rows * small, width), f32)]
    outs += [((rows + 2 * small_rows * small, width), bf16)] * (count - 1)
    got = swap_with(sent, "tp", 1)
    pieces = in_vmem(pair_with_small if small else pair_kernel, outs, kept, got)
    return [pieces[0]] + [swap_with(pieces[k], "ctx", k) for k in range(1, count)]


def per_device(
    inputs,
    cotangent,
    mixer_matrix,
    ffn_weight,
    conv_weight,
    norm_gains,
    mixer_first,
    mixer_second,
    ffn_first,
    ffn_second,
    conv_first,
    conv_second,
    gain_first,
    gain_second,
):
    shard_count = lax.axis_size("shard")
    ctx_count = lax.axis_size("ctx")
    tp_count = lax.axis_size("tp")
    seq_count, tok_count, width = inputs.shape
    assert seq_count == 1 and tp_count == 2
    half = tok_count // tp_count
    seq_len = tok_count * ctx_count

    half_shape, half_sent = ((half, width), f32), ((half, width), bf16)

    def both_halves(mine):
        other = swap_with(mine, "tp", 1)
        whole = ((1, tok_count, width), mine.dtype)
        return in_vmem(join_rows, [whole], mine, other)[0]

    x_half = in_vmem(own_rows, [half_sent], inputs)[0]
    x_pieces = spread_rows(x_half)
    block = mixer_matrix.shape[0]
    mixer_own = in_vmem(prepare_mixer, [((4, block, width), bf16)], mixer_matrix)[0]
    mixer_parts = [mixer_own] + [swap_with(mixer_own, "shard", k) for k in range(1, shard_count)]
    ffn_block = ffn_weight.shape[0]
    ffn_own = in_vmem(
        prepare_ffn, [((3, ffn_block, width // 2), bf16)] * 2, ffn_weight.transpose(1, 0, 2)
    )
    ffn_halves = across_shard(ffn_own)
    ffn_parts = [half for halves in ffn_halves for half in halves]
    g_half = in_vmem(own_rows, [half_sent], cotangent)[0]
    g_pieces = spread_rows(g_half)

    channels, hidden = block * shard_count, ffn_block * shard_count
    mine_count = seq_len // 2
    parted = [((mine_count, width), f32), ((mine_count, width), bf16)]

    h_one, mixer_w, projected, gated, taps, kept, sent = in_vmem(
        functools.partial(mixer_forward, ctx_count, shard_count),
        [
            ((seq_len, width), bf16),
            ((4 * channels, width), bf16),
            ((seq_len, 3 * channels), f32),
            ((seq_len, channels), bf16),
            ((3, channels), f32),
        ]
        + parted,
        *x_pieces,
        *mixer_parts,
        norm_gains,
        conv_weight,
        flops=8 * seq_len * channels * width,
    )
    residual, normed_two, h_two_own = in_vmem(
        second_norm,
        [half_shape, half_shape, half_sent],
        *collect_rows(kept, sent),
        x_half,
        norm_gains,
    )

    hidden_rows = ((seq_len, hidden), bf16)
    g_all, gate_up_w, down_w = in_vmem(
        functools.partial(ffn_gather, ctx_count),
        [
            ((seq_len, width), bf16),
            ((2 * hidden, width), bf16),
            ((hidden, width), bf16),
        ],
        *g_pieces,
        *ffn_parts,
    )
    h_two, act, grad_gate, grad_up, kept, sent = in_vmem(
        functools.partial(ffn_rows, ctx_count),
        [((seq_len, width), bf16), hidden_rows, hidden_rows, hidden_rows] + parted,
        *spread_rows(h_two_own),
        g_all,
        gate_up_w,
        down_w,
        flops=10 * seq_len * hidden * width,
    )
    grad_resid, grad_mix_own, gain_two_part = in_vmem(
        second_norm_backward,
        [half_shape, half_sent, ((1, width), f32)],
        *collect_rows(kept, sent),
        residual,
        normed_two,
        g_half,
        norm_gains,
    )
    kept, sent = in_vmem(ffn_down, parted, act, down_w, flops=2 * seq_len * hidden * width)
    ffn_pieces = collect_rows(kept, sent)
    ffn_terms = in_vmem(
        functools.partial(ffn_weight_grads, shard_count),
        [((3, ffn_block, width), f32)] + [((3, ffn_block, width), bf16)] * (shard_count - 1),
        grad_gate,
        grad_up,
        act,
        h_two,
        g_all,
        flops=6 * seq_len * hidden * width,
    )
    ffn_got = [swap_with(ffn_terms[k], "shard", k) for k in range(1, shard_count)]

    grad_mix_all, grad_triple, kept, sent = in_vmem(
        functools.partial(mixer_backward, ctx_count, shard_count),
        [
            ((seq_len, width), bf16),
            ((seq_len, 3 * channels), bf16),
            ((mine_count + small_rows, width), f32),
            ((mine_count + 2 * small_rows, width), bf16),
        ],
        *spread_rows(grad_mix_own),
        h_one,
        mixer_w,
        projected,
        norm_gains,
        taps,
        gain_two_part,
        scratch=[pltpu.VMEM((small_rows, width), f32)],
        flops=8 * seq_len * channels * width,
    )
    in_pieces = collect_rows(kept, sent, small=True)
    mixer_terms = in_vmem(
        functools.partial(mixer_weight_grads, shard_count),
        [((4, block, width), f32)] + [((4, block, width), bf16)] * (shard_count - 1),
        grad_triple,
        h_one,
        gated,
        grad_mix_all,
        flops=8 * seq_len * channels * width,
    )
    mixer_got = [swap_with(mixer_terms[k], "shard", k) for k in range(1, shard_count)]
    ffn_news = in_vmem(
        functools.partial(ffn_adam, shard_count),
        [((3, ffn_block, width), f32)] * 4,
        ffn_terms[0],
        *ffn_got,
        *(value.transpose(1, 0, 2) for value in (ffn_weight, ffn_first, ffn_second)),
    )
    ffn_grad, ffn_new, ffn_first_new, ffn_second_new = (
        value.transpose(1, 0, 2) for value in ffn_news
    )
    out_own = in_vmem(output_kernel, [half_sent], *ffn_pieces, residual)[0]
    output = both_halves(out_own)
    input_grad, small = in_vmem(
        first_norm_backward,
        [half_shape, ((small_rows, width), f32)],
        *in_pieces,
        x_half,
        grad_resid,
        norm_gains,
    )
    input_grad = both_halves(input_grad)
    (
        gain_grad,
        gain_new,
        gain_first_new,
        gain_second_new,
        conv_grad,
        conv_new,
        conv_first_new,
        conv_second_new,
    ) = in_vmem(
        functools.partial(small_adam, shard_count),
        [(norm_gains.shape, f32)] * 4 + [(conv_weight.shape, f32)] * 4,
        small,
        *(swap_with(small, "shard", k) for k in range(1, shard_count)),
        norm_gains,
        gain_first,
        gain_second,
        conv_weight,
        conv_first,
        conv_second,
    )
    mixer_grad, mixer_new, mixer_first_new, mixer_second_new = in_vmem(
        functools.partial(mixer_adam, shard_count),
        [(mixer_matrix.shape, f32)] * 4,
        mixer_terms[0],
        *mixer_got,
        mixer_matrix,
        mixer_first,
        mixer_second,
    )
    return (
        output,
        input_grad,
        mixer_grad,
        ffn_grad,
        conv_grad,
        gain_grad,
        mixer_new,
        ffn_new,
        conv_new,
        gain_new,
        mixer_first_new,
        mixer_second_new,
        ffn_first_new,
        ffn_second_new,
        conv_first_new,
        conv_second_new,
        gain_first_new,
        gain_second_new,
    )


def solution(mesh):
    tokens = P("shard", "ctx", None)
    rows = P(("shard", "ctx", "tp"), None, None)
    in_specs = (tokens, tokens, rows, rows, P(), P(), rows, rows, rows, rows, P(), P(), P(), P())
    out_specs = (
        (tokens, tokens, rows, rows, P(), P(), rows, rows, P(), P())
        + (rows, rows, rows, rows)
        + (P(), P(), P(), P())
    )

    return jax.shard_map(
        per_device, mesh=mesh, in_specs=in_specs, out_specs=out_specs, check_vma=False
    )
```

```python
import functools

import jax
import jax.numpy as jnp
from jax import lax
from jax.experimental import pallas as pl
from jax.experimental.pallas import tpu as pltpu
from jax.sharding import PartitionSpec as P


STEP = 10


norm_eps = 1e-05
beta_first = 0.9
beta_second = 0.999
adam_eps = 1e-08
matrix_rate = 0.02
small_rate = 0.25
decay_rate = 0.1
small_rows = 8

bf16 = jnp.bfloat16
f32 = jnp.float32


def norm_backward(grad_normed, normed, scale):
    return scale * (grad_normed - normed * jnp.mean(grad_normed * normed, axis=-1, keepdims=True))


def adam_update(weight, gradient, first, second, rate, decay):
    first_new = beta_first * first + (1.0 - beta_first) * gradient
    second_new = beta_second * second + (1.0 - beta_second) * gradient * gradient
    first_hat = first_new / (1.0 - beta_first**STEP)
    second_hat = second_new / (1.0 - beta_second**STEP)
    weight_new = weight - rate * (first_hat / (jnp.sqrt(second_hat) + adam_eps) + decay * weight)
    return (weight_new, first_new, second_new)


def partner_of(index, step, count):
    assert count & (count - 1) == 0
    return index ^ step


def swap_with(value, axis, step):
    count = lax.axis_size(axis)
    return lax.ppermute(
        value, axis, [(i, partner_of(i, step, count)) for i in range(count)]
    )


def tree_sum(values):
    while len(values) > 1:
        values = [a + b for a, b in zip(values[::2], values[1::2])]
    return values[0]


def across_shard(halves):
    count = lax.axis_size("shard")
    pieces = [list(halves)]
    for k in range(1, count):
        low, high = k & -k, 1 << (k.bit_length() - 1)
        pieces.append(
            [swap_with(pieces[k ^ via][j], "shard", via) for j, via in enumerate((low, high))]
        )
    return pieces


def owners_terms(terms):
    count = lax.axis_size("shard")
    if count != 4:
        return [[swap_with(terms[k - 1][j], "shard", k) for k in range(1, count)] for j in range(2)]
    (near_a, near_b), (next_a, next_b), (far_a, far_b) = terms
    passed_a = swap_with(far_a, "shard", 1)
    passed_b = swap_with(far_b, "shard", 2)
    came_near_a = swap_with(near_a, "shard", 1)
    came_next_b = swap_with(next_b, "shard", 2)
    shape = [(near_a.shape, bf16)]
    joint_a, joint_b = in_vmem(add_pairs, shape * 2, next_a, passed_a, near_b, passed_b)
    came_next_a = swap_with(joint_a, "shard", 2)
    came_near_b = swap_with(joint_b, "shard", 1)
    return [[came_near_a, came_next_a], [came_near_b, came_next_b]]


def add_pairs(*refs):
    for j, out_ref in enumerate(refs[2 * (len(refs) // 3) :]):
        total = refs[2 * j][...].astype(f32) + refs[2 * j + 1][...].astype(f32)
        out_ref[...] = total.astype(out_ref.dtype)


def spread_rows(own):
    count = lax.axis_size("ctx")
    mine = [own]
    for k in range(1, count):
        if k == 1 or k % 2 == 0:
            mine.append(swap_with(own, "ctx", k))
        else:
            mine.append(swap_with(mine[k - 1], "ctx", 1))
    return mine + [swap_with(piece, "tp", 1) for piece in mine]


def in_vmem(body, outs, *operands, scratch=(), flops=0, mib=16):
    shapes = [jax.ShapeDtypeStruct(shape, dtype) for shape, dtype in outs]
    moved = sum(x.size * x.dtype.itemsize for x in (*operands, *shapes))
    return pl.pallas_call(
        body,
        out_shape=shapes,
        in_specs=[pl.BlockSpec(memory_space=pltpu.VMEM)] * len(operands),
        out_specs=[pl.BlockSpec(memory_space=pltpu.VMEM)] * len(shapes),
        scratch_shapes=list(scratch),
        compiler_params=pltpu.CompilerParams(vmem_limit_bytes=mib << 20),
        cost_estimate=pl.CostEstimate(flops=flops, bytes_accessed=moved, transcendentals=0),
    )(*operands)


def by_rows(rows, weight):
    return lax.dot_general(rows, weight, (((1,), (1,)), ((), ())), preferred_element_type=f32)


def down_rows(left, right):
    return lax.dot_general(left, right, (((0,), (0,)), ((), ())), preferred_element_type=f32)


def block_start(step, core, rows):
    return pl.multiple_of((2 * jnp.bitwise_xor(lax.axis_index("ctx"), step) + core) * rows, rows)


def delayed(values, steps):
    length = values.shape[0]
    rolled = pltpu.roll(values, steps % length, 0)
    row = lax.broadcasted_iota(jnp.int32, values.shape, 0)
    kept = row >= steps if steps > 0 else row < length + steps
    return jnp.where(kept, rolled, 0.0)


def convolved(b_part, x_part, taps):
    product = b_part * x_part
    one, two = delayed(product, 1), delayed(product, 2)
    return product, one, two, taps[0:1] * two + taps[1:2] * one + taps[2:3] * product


def own_columns(groups, block, shape):
    row = lax.broadcasted_iota(jnp.int32, shape, 0)
    ahead = lax.broadcasted_iota(jnp.int32, shape, 1) - row
    stride = shape[1] // groups
    found = jnp.zeros(shape, f32)
    group_at = lax.axis_index("shard")
    within = lax.axis_index("ctx") * lax.axis_size("tp") + lax.axis_index("tp")
    for k in range(groups):
        base = jnp.bitwise_xor(group_at, k) * stride + (within - k) * block
        inside = (row >= k * block) & (row < (k + 1) * block)
        found = jnp.where(inside & (ahead == base), 1.0, found)
    return found


def mixer_forward(count, groups, *refs):
    pieces, parts = refs[: 2 * count], refs[2 * count : 2 * count + groups]
    gain_ref, conv_ref, h_ref, w_ref, p_ref, y_ref, taps_ref, keep_ref, send_ref = refs[
        2 * count + groups :
    ]
    rows = pieces[0].shape[0]
    block, channels = parts[0].shape[1], y_ref.shape[1]
    core = lax.axis_index("tp")
    taps_ref[...] = lax.dot_general(
        conv_ref[...],
        own_columns(groups, block, (channels, conv_ref.shape[1])),
        (((1,), (1,)), ((), ())),
        precision=lax.Precision.HIGHEST,
        preferred_element_type=f32,
    )
    for k in range(4):
        for s in range(groups):
            w_ref[k * channels + s * block : k * channels + (s + 1) * block, :] = parts[s][k]
    gain = gain_ref[0:1, :]
    for j in range(2 * count):
        x = pieces[j][...].astype(f32)
        scale = lax.rsqrt(jnp.mean(x * x, axis=-1, keepdims=True) + norm_eps)
        side = core if j < count else 1 - core
        h_ref[pl.ds(block_start(j % count, side, rows), rows), :] = (x * scale * gain).astype(bf16)
    p_ref[...] = by_rows(h_ref[...], w_ref[: 3 * channels, :])
    in_b, in_c = p_ref[:, :channels], p_ref[:, channels : 2 * channels]
    in_x = p_ref[:, 2 * channels :]
    mixed = convolved(in_b, in_x, taps_ref[...])[3]
    y_ref[...] = (in_c * mixed).astype(bf16)
    out_w = w_ref[3 * channels :, :]
    for side, out_ref in ((1 - core, send_ref), (core, keep_ref)):
        starts = [block_start(k, side, rows) for k in range(count)]
        rows_of = [y_ref[pl.ds(at, rows), :] for at in starts]
        part = jnp.dot(jnp.concatenate(rows_of, axis=0), out_w, preferred_element_type=f32)
        out_ref[...] = part.astype(out_ref.dtype)


def halves_of(values):
    coarse = values.astype(bf16)
    return coarse, (values - coarse.astype(f32)).astype(bf16)


def whole_of(ref, at):
    rows = small_rows
    return ref[at : at + rows, :].astype(f32) + ref[at + rows : at + 2 * rows, :].astype(f32)


def mixer_backward(count, groups, *refs):
    pieces = refs[: 2 * count]
    h_ref, w_ref, p_ref, gain_ref, taps_ref, gain_two_ref = refs[2 * count : 2 * count + 6]
    dm_ref, dp_ref, keep_ref, send_ref, small_ref = refs[2 * count + 6 :]
    rows, side_rows = pieces[0].shape[0], count * pieces[0].shape[0]
    channels = taps_ref.shape[1]
    core = lax.axis_index("tp")
    for j in range(2 * count):
        side = core if j < count else 1 - core
        dm_ref[pl.ds(block_start(j % count, side, rows), rows), :] = pieces[j][...]
    grad_gated = by_rows(dm_ref[...], w_ref[3 * channels :, :])
    in_b, in_c = p_ref[:, :channels], p_ref[:, channels : 2 * channels]
    in_x = p_ref[:, 2 * channels :]
    taps = taps_ref[...]
    product, one, two, mixed = convolved(in_b, in_x, taps)
    grad_mixed = grad_gated * in_c
    next_one, next_two = delayed(grad_mixed, -1), delayed(grad_mixed, -2)
    grad_prod = taps[0:1] * next_two + taps[1:2] * next_one + taps[2:3] * grad_mixed
    dp_ref[:, :channels] = (grad_prod * in_x).astype(bf16)
    dp_ref[:, channels : 2 * channels] = (grad_gated * mixed).astype(bf16)
    dp_ref[:, 2 * channels :] = (grad_prod * in_b).astype(bf16)
    tap_sums = [
        jnp.sum(grad_mixed * shifted, axis=0, keepdims=True) for shifted in (two, one, product)
    ]
    small_ref[...] = jnp.zeros(small_ref.shape, f32)
    small_ref[2:5, :] = jnp.dot(
        jnp.concatenate(tap_sums, axis=0),
        own_columns(groups, channels // groups, (channels, h_ref.shape[1])),
        precision=lax.Precision.HIGHEST,
        preferred_element_type=f32,
    )
    small_ref[1:2, :] = gain_two_ref[...]
    gain_sum = jnp.zeros((1, gain_ref.shape[1]), f32)
    for side, out_ref in ((1 - core, send_ref), (core, keep_ref)):
        starts = [block_start(k, side, rows) for k in range(count)]
        grads = jnp.concatenate([dp_ref[pl.ds(at, rows), :] for at in starts], axis=0)
        part = jnp.dot(grads, w_ref[: 3 * channels, :], preferred_element_type=f32)
        out_ref[:side_rows, :] = part.astype(out_ref.dtype)
        normed = jnp.concatenate([h_ref[pl.ds(at, rows), :] for at in starts], axis=0)
        gain_sum = gain_sum + jnp.sum(part * normed.astype(f32), axis=0, keepdims=True)
    small_ref[0:1, :] = gain_sum / gain_ref[0:1, :]
    coarse, fine = halves_of(small_ref[...])
    send_ref[side_rows:, :] = jnp.concatenate([coarse, fine], axis=0)
    keep_ref[side_rows:, :] = coarse.astype(f32) + fine.astype(f32)


def mixer_weight_grads(groups, dp_ref, h_ref, y_ref, dm_ref, *outs):
    block = outs[0].shape[1]
    channels = y_ref.shape[1]
    inner = down_rows(dp_ref[...], h_ref[...])
    outer = down_rows(y_ref[...], dm_ref[...])
    for s in range(groups):
        for k in range(3):
            at = k * channels + s * block
            outs[s][k] = inner[at : at + block].astype(outs[s].dtype)
        outs[s][3] = outer[s * block : (s + 1) * block].astype(outs[s].dtype)


def ffn_gather(count, *refs):
    *pieces, g_ref, w_ref, down_ref = refs
    g_pieces, parts = pieces[: 2 * count], pieces[2 * count :]
    rows, hidden = g_pieces[0].shape[0], down_ref.shape[0]
    for j in range(2 * count):
        g_ref[j * rows : (j + 1) * rows, :] = g_pieces[j][...]
    block, columns = parts[0].shape[1:]
    for j, part in enumerate(parts):
        at, side = (j // 2) * block, slice((j % 2) * columns, (j % 2 + 1) * columns)
        w_ref[at : at + block, side] = part[0]
        w_ref[hidden + at : hidden + at + block, side] = part[1]
        down_ref[at : at + block, side] = part[2]


def ffn_rows(count, *refs):
    pieces = refs[: 2 * count]
    g_ref, w_ref, down_ref, h_ref, act_ref, gate_ref, up_ref, keep_ref, send_ref = refs[2 * count :]
    rows, hidden = pieces[0].shape[0], down_ref.shape[0]
    for j in range(2 * count):
        h_ref[j * rows : (j + 1) * rows, :] = pieces[j][...]
    side_rows = count * rows
    for at, out_ref in ((side_rows, send_ref), (0, keep_ref)):
        these = slice(at, at + side_rows)
        gate = by_rows(h_ref[these, :], w_ref[:hidden, :])
        up = by_rows(h_ref[these, :], w_ref[hidden:, :])
        sigmoid = jax.nn.sigmoid(gate)
        gate_act = gate * sigmoid
        act_ref[these, :] = (gate_act * up).astype(bf16)
        grad_act = by_rows(g_ref[these, :], down_ref[...])
        up_ref[these, :] = (grad_act * gate_act).astype(bf16)
        gate_ref[these, :] = (
            grad_act * up * sigmoid * (1.0 + gate * (1.0 - sigmoid))
        ).astype(bf16)
        part = jnp.dot(gate_ref[these, :], w_ref[:hidden, :], preferred_element_type=f32)
        part = part + jnp.dot(up_ref[these, :], w_ref[hidden:, :], preferred_element_type=f32)
        out_ref[...] = part.astype(out_ref.dtype)


def ffn_down(act_ref, down_ref, keep_ref, send_ref):
    half = keep_ref.shape[0]
    for at, out_ref in ((half, send_ref), (0, keep_ref)):
        part = jnp.dot(act_ref[at : at + half, :], down_ref[...], preferred_element_type=f32)
        out_ref[...] = part.astype(out_ref.dtype)


def ffn_weight_grads(gate_ref, up_ref, act_ref, h_ref, g_ref, *outs):
    own_ref, halves = outs[0], outs[1:]
    block, columns = own_ref.shape[1], halves[0].shape[2]
    for k, (left, right) in enumerate(((gate_ref, h_ref), (up_ref, h_ref), (act_ref, g_ref))):
        term = down_rows(left[...], right[...])
        own_ref[k] = term[:block]
        for j, out_ref in enumerate(halves):
            at, side = (1 + j // 2) * block, (j % 2) * columns
            out_ref[k] = term[at : at + block, side : side + columns].astype(bf16)


def ffn_adam(half_parts, *refs):
    own_ref, parts = refs[0], refs[1 : 1 + 2 * half_parts]
    weight, first, second, grad_out, *outs = refs[1 + 2 * half_parts :]
    columns = parts[0].shape[2]
    for k in range(3):
        for j in range(2):
            side = slice(j * columns, (j + 1) * columns)
            grad = own_ref[k, :, side]
            for part in parts[j * half_parts : (j + 1) * half_parts]:
                grad = grad + part[k].astype(f32)
            grad_out[k, :, side] = grad
            news = adam_update(
                weight[k, :, side],
                grad,
                first[k, :, side],
                second[k, :, side],
                matrix_rate,
                decay_rate,
            )
            for out, new in zip(outs, news):
                out[k, :, side] = new


def mixer_adam(groups, *refs):
    own_ref, *parts = refs[:groups]
    weight, first, second, grad_out, weight_out, first_out, second_out = refs[groups:]
    for k in range(4):
        grad = own_ref[k]
        for part in parts:
            grad = grad + part[k].astype(f32)
        news = adam_update(
            weight[:, k, :], grad, first[:, k, :], second[:, k, :], matrix_rate, decay_rate
        )
        grad_out[:, k, :] = grad
        for out, new in zip((weight_out, first_out, second_out), news):
            out[:, k, :] = new


def pair_kernel(kept_ref, got_ref, *outs):
    rows = outs[0].shape[0]
    for k, out_ref in enumerate(outs):
        at = slice(k * rows, (k + 1) * rows)
        out_ref[...] = (kept_ref[at, :] + got_ref[at, :].astype(f32)).astype(out_ref.dtype)


def pair_with_small(kept_ref, got_ref, *outs):
    rows = outs[0].shape[0] - small_rows
    count = len(outs)
    small = kept_ref[count * rows :, :] + whole_of(got_ref, count * rows)
    rounded = small.astype(bf16)
    for k, out_ref in enumerate(outs):
        at = slice(k * rows, (k + 1) * rows)
        pair = kept_ref[at, :] + got_ref[at, :].astype(f32)
        out_ref[:rows, :] = pair.astype(out_ref.dtype)
        out_ref[rows:, :] = rounded.astype(out_ref.dtype)


def total_of(own_ref, got_refs, rows=None):
    total = own_ref[:rows, :]
    for got in got_refs:
        total = total + got[:rows, :].astype(f32)
    return total


def own_rows(rows_ref, out_ref):
    count = out_ref.shape[0]
    start = pl.multiple_of(lax.axis_index("tp") * count, count)
    out_ref[...] = rows_ref[0, pl.ds(start, count), :]


def join_rows(mine_ref, other_ref, out_ref):
    count, core = mine_ref.shape[0], lax.axis_index("tp")
    out_ref[0, pl.ds(pl.multiple_of(core * count, count), count), :] = mine_ref[...]
    out_ref[0, pl.ds(pl.multiple_of((1 - core) * count, count), count), :] = other_ref[...]


def prepare_ffn(weight_ref, *outs):
    columns = outs[0].shape[2]
    for j, out_ref in enumerate(outs):
        out_ref[...] = weight_ref[:, :, j * columns : (j + 1) * columns].astype(bf16)


def prepare_mixer(weight_ref, out_ref):
    for k in range(4):
        out_ref[k] = weight_ref[:, k, :].astype(bf16)


def second_norm(*refs):
    own_ref, *got = refs[:-5]
    x_ref, gain_ref, resid_ref, normed_ref, h_ref = refs[-5:]
    residual = x_ref[...].astype(f32) + total_of(own_ref, got)
    resid_ref[...] = residual
    normed = residual * lax.rsqrt(jnp.mean(residual * residual, axis=-1, keepdims=True) + norm_eps)
    normed_ref[...] = normed
    h_ref[...] = (normed * gain_ref[1:2, :]).astype(bf16)


def second_norm_backward(*refs):
    own_ref, *got = refs[:-7]
    resid_ref, normed_ref, g_ref, gain_ref, grad_ref, dm_ref, gain_part_ref = refs[-7:]
    grad_h = total_of(own_ref, got)
    normed, residual = normed_ref[...], resid_ref[...]
    scale = lax.rsqrt(jnp.mean(residual * residual, axis=-1, keepdims=True) + norm_eps)
    grad = g_ref[...].astype(f32) + norm_backward(grad_h * gain_ref[1:2, :], normed, scale)
    grad_ref[...] = grad
    dm_ref[...] = grad.astype(bf16)
    gain_part_ref[...] = jnp.sum(grad_h * normed, axis=0, keepdims=True)


def first_norm_backward(*refs):
    own_ref, *got = refs[:-5]
    x_ref, grad_ref, gain_ref, out_ref, small_ref = refs[-5:]
    rows = x_ref.shape[0]
    x = x_ref[...].astype(f32)
    scale = lax.rsqrt(jnp.mean(x * x, axis=-1, keepdims=True) + norm_eps)
    out_ref[...] = grad_ref[...] + norm_backward(
        total_of(own_ref, got, rows) * gain_ref[0:1, :], x * scale, scale
    )
    small_ref[...] = tree_sum([ref[rows:, :].astype(f32) for ref in (own_ref, *got)])


def small_adam(groups, *refs):
    pieces, operands, outs = refs[:groups], refs[groups : groups + 6], refs[groups + 6 :]
    total = tree_sum([piece[...] for piece in pieces])
    for which, grad in enumerate((total[0:2], total[2:5])):
        weight, first, second = (ref[...] for ref in operands[3 * which : 3 * which + 3])
        news = adam_update(weight, grad, first, second, small_rate, 0.0)
        for out, value in zip(outs[4 * which : 4 * which + 4], (grad, *news)):
            out[...] = value


def output_kernel(*refs):
    own_ref, *got = refs[:-2]
    resid_ref, out_ref = refs[-2:]
    out_ref[...] = (resid_ref[...] + total_of(own_ref, got)).astype(out_ref.dtype)


def collect_rows(kept, sent, small=False, passed=False):
    count = lax.axis_size("ctx")
    width = kept.shape[1]
    rows = (kept.shape[0] - small_rows * small) // count
    outs = [((rows + small_rows * small, width), f32)]
    outs += [((rows + small_rows * small, width), bf16)] * (count - 1)
    got = swap_with(sent, "tp", 1)
    pieces = in_vmem(pair_with_small if small else pair_kernel, outs, kept, got)
    if not passed or count != 4:
        return [pieces[0]] + [swap_with(pieces[k], "ctx", k) for k in range(1, count)]
    came = swap_with(pieces[3], "ctx", 1)
    near = swap_with(pieces[1], "ctx", 1)
    joint = in_vmem(add_pairs, outs[2:3], pieces[2], came)
    return [pieces[0], near, swap_with(joint[0], "ctx", 2)]


def per_device(
    inputs,
    cotangent,
    mixer_matrix,
    ffn_weight,
    conv_weight,
    norm_gains,
    mixer_first,
    mixer_second,
    ffn_first,
    ffn_second,
    conv_first,
    conv_second,
    gain_first,
    gain_second,
):
    shard_count = lax.axis_size("shard")
    ctx_count = lax.axis_size("ctx")
    tp_count = lax.axis_size("tp")
    seq_count, tok_count, width = inputs.shape
    assert seq_count == 1 and tp_count == 2
    half = tok_count // tp_count
    seq_len = tok_count * ctx_count

    half_shape, half_sent = ((half, width), f32), ((half, width), bf16)

    def both_halves(mine):
        other = swap_with(mine, "tp", 1)
        whole = ((1, tok_count, width), mine.dtype)
        return in_vmem(join_rows, [whole], mine, other)[0]

    x_half = in_vmem(own_rows, [half_sent], inputs)[0]
    x_pieces = spread_rows(x_half)
    block = mixer_matrix.shape[0]
    mixer_own = in_vmem(prepare_mixer, [((4, block, width), bf16)], mixer_matrix)[0]
    mixer_parts = [mixer_own] + [swap_with(mixer_own, "shard", k) for k in range(1, shard_count)]
    ffn_block = ffn_weight.shape[0]
    ffn_own = in_vmem(
        prepare_ffn, [((3, ffn_block, width // 2), bf16)] * 2, ffn_weight.transpose(1, 0, 2)
    )
    ffn_halves = across_shard(ffn_own)
    ffn_parts = [half for halves in ffn_halves for half in halves]
    g_half = in_vmem(own_rows, [half_sent], cotangent)[0]
    g_pieces = spread_rows(g_half)

    channels, hidden = block * shard_count, ffn_block * shard_count
    mine_count = seq_len // 2
    parted = [((mine_count, width), f32), ((mine_count, width), bf16)]

    h_one, mixer_w, projected, gated, taps, kept, sent = in_vmem(
        functools.partial(mixer_forward, ctx_count, shard_count),
        [
            ((seq_len, width), bf16),
            ((4 * channels, width), bf16),
            ((seq_len, 3 * channels), f32),
            ((seq_len, channels), bf16),
            ((3, channels), f32),
        ]
        + parted,
        *x_pieces,
        *mixer_parts,
        norm_gains,
        conv_weight,
        flops=8 * seq_len * channels * width,
    )
    residual, normed_two, h_two_own = in_vmem(
        second_norm,
        [half_shape, half_shape, half_sent],
        *collect_rows(kept, sent),
        x_half,
        norm_gains,
    )

    hidden_rows = ((seq_len, hidden), bf16)
    g_all, gate_up_w, down_w = in_vmem(
        functools.partial(ffn_gather, ctx_count),
        [
            ((seq_len, width), bf16),
            ((2 * hidden, width), bf16),
            ((hidden, width), bf16),
        ],
        *g_pieces,
        *ffn_parts,
    )
    h_two, act, grad_gate, grad_up, kept, sent = in_vmem(
        functools.partial(ffn_rows, ctx_count),
        [((seq_len, width), bf16), hidden_rows, hidden_rows, hidden_rows] + parted,
        *spread_rows(h_two_own),
        g_all,
        gate_up_w,
        down_w,
        flops=10 * seq_len * hidden * width,
    )
    grad_resid, grad_mix_own, gain_two_part = in_vmem(
        second_norm_backward,
        [half_shape, half_sent, ((1, width), f32)],
        *collect_rows(kept, sent),
        residual,
        normed_two,
        g_half,
        norm_gains,
    )
    kept, sent = in_vmem(ffn_down, parted, act, down_w, flops=2 * seq_len * hidden * width)
    ffn_pieces = collect_rows(kept, sent, passed=True)
    ffn_terms = in_vmem(
        ffn_weight_grads,
        [((3, ffn_block, width), f32)]
        + [((3, ffn_block, width // 2), bf16)] * (2 * (shard_count - 1)),
        grad_gate,
        grad_up,
        act,
        h_two,
        g_all,
        flops=6 * seq_len * hidden * width,
    )
    ffn_got = owners_terms(list(zip(ffn_terms[1::2], ffn_terms[2::2])))

    grad_mix_all, grad_triple, kept, sent = in_vmem(
        functools.partial(mixer_backward, ctx_count, shard_count),
        [
            ((seq_len, width), bf16),
            ((seq_len, 3 * channels), bf16),
            ((mine_count + small_rows, width), f32),
            ((mine_count + 2 * small_rows, width), bf16),
        ],
        *spread_rows(grad_mix_own),
        h_one,
        mixer_w,
        projected,
        norm_gains,
        taps,
        gain_two_part,
        scratch=[pltpu.VMEM((small_rows, width), f32)],
        flops=8 * seq_len * channels * width,
    )
    in_pieces = collect_rows(kept, sent, small=True)
    mixer_terms = in_vmem(
        functools.partial(mixer_weight_grads, shard_count),
        [((4, block, width), f32)] + [((4, block, width), bf16)] * (shard_count - 1),
        grad_triple,
        h_one,
        gated,
        grad_mix_all,
        flops=8 * seq_len * channels * width,
    )
    mixer_got = [swap_with(mixer_terms[k], "shard", k) for k in range(1, shard_count)]
    ffn_news = in_vmem(
        functools.partial(ffn_adam, len(ffn_got[0])),
        [((3, ffn_block, width), f32)] * 4,
        ffn_terms[0],
        *ffn_got[0],
        *ffn_got[1],
        *(value.transpose(1, 0, 2) for value in (ffn_weight, ffn_first, ffn_second)),
    )
    ffn_grad, ffn_new, ffn_first_new, ffn_second_new = (
        value.transpose(1, 0, 2) for value in ffn_news
    )
    out_own = in_vmem(output_kernel, [half_sent], *ffn_pieces, residual)[0]
    output = both_halves(out_own)
    input_grad, small = in_vmem(
        first_norm_backward,
        [half_shape, ((small_rows, width), f32)],
        *in_pieces,
        x_half,
        grad_resid,
        norm_gains,
    )
    input_grad = both_halves(input_grad)
    (
        gain_grad,
        gain_new,
        gain_first_new,
        gain_second_new,
        conv_grad,
        conv_new,
        conv_first_new,
        conv_second_new,
    ) = in_vmem(
        functools.partial(small_adam, shard_count),
        [(norm_gains.shape, f32)] * 4 + [(conv_weight.shape, f32)] * 4,
        small,
        *(swap_with(small, "shard", k) for k in range(1, shard_count)),
        norm_gains,
        gain_first,
        gain_second,
        conv_weight,
        conv_first,
        conv_second,
    )
    mixer_grad, mixer_new, mixer_first_new, mixer_second_new = in_vmem(
        functools.partial(mixer_adam, shard_count),
        [(mixer_matrix.shape, f32)] * 4,
        mixer_terms[0],
        *mixer_got,
        mixer_matrix,
        mixer_first,
        mixer_second,
    )
    return (
        output,
        input_grad,
        mixer_grad,
        ffn_grad,
        conv_grad,
        gain_grad,
        mixer_new,
        ffn_new,
        conv_new,
        gain_new,
        mixer_first_new,
        mixer_second_new,
        ffn_first_new,
        ffn_second_new,
        conv_first_new,
        conv_second_new,
        gain_first_new,
        gain_second_new,
    )


def solution(mesh):
    tokens = P("shard", "ctx", None)
    rows = P(("shard", "ctx", "tp"), None, None)
    in_specs = (tokens, tokens, rows, rows, P(), P(), rows, rows, rows, rows, P(), P(), P(), P())
    out_specs = (
        (tokens, tokens, rows, rows, P(), P(), rows, rows, P(), P())
        + (rows, rows, rows, rows)
        + (P(), P(), P(), P())
    )

    return jax.shard_map(
        per_device, mesh=mesh, in_specs=in_specs, out_specs=out_specs, check_vma=False
    )
```

```python
import functools

import jax
import jax.numpy as jnp
from jax import lax
from jax.experimental import pallas as pl
from jax.experimental.pallas import tpu as pltpu
from jax.sharding import PartitionSpec as P


STEP = 10


norm_eps = 1e-05
beta_first = 0.9
beta_second = 0.999
adam_eps = 1e-08
matrix_rate = 0.02
small_rate = 0.25
decay_rate = 0.1
small_rows = 8

bf16 = jnp.bfloat16
f32 = jnp.float32


def norm_backward(grad_normed, normed, scale):
    return scale * (grad_normed - normed * jnp.mean(grad_normed * normed, axis=-1, keepdims=True))


def adam_update(weight, gradient, first, second, rate, decay):
    first_new = beta_first * first + (1.0 - beta_first) * gradient
    second_new = beta_second * second + (1.0 - beta_second) * gradient * gradient
    first_hat = first_new / (1.0 - beta_first**STEP)
    second_hat = second_new / (1.0 - beta_second**STEP)
    weight_new = weight - rate * (first_hat / (jnp.sqrt(second_hat) + adam_eps) + decay * weight)
    return (weight_new, first_new, second_new)


def partner_of(index, step, count):
    assert count & (count - 1) == 0
    return index ^ step


def swap_with(value, axis, step):
    count = lax.axis_size(axis)
    return lax.ppermute(
        value, axis, [(i, partner_of(i, step, count)) for i in range(count)]
    )


def tree_sum(values):
    while len(values) > 1:
        values = [a + b for a, b in zip(values[::2], values[1::2])]
    return values[0]


def across_shard(halves):
    count = lax.axis_size("shard")
    pieces = [list(halves)]
    for k in range(1, count):
        low, high = k & -k, 1 << (k.bit_length() - 1)
        pieces.append(
            [swap_with(pieces[k ^ via][j], "shard", via) for j, via in enumerate((low, high))]
        )
    return pieces


def owners_terms(terms):
    count = lax.axis_size("shard")
    if count != 4:
        return [[swap_with(terms[k - 1][j], "shard", k) for k in range(1, count)] for j in range(2)]
    (near_a, near_b), (next_a, next_b), (far_a, far_b) = terms
    passed_a = swap_with(far_a, "shard", 1)
    passed_b = swap_with(far_b, "shard", 2)
    came_near_a = swap_with(near_a, "shard", 1)
    came_next_b = swap_with(next_b, "shard", 2)
    shape = [(near_a.shape, bf16)]
    joint_a, joint_b = in_vmem(add_pairs, shape * 2, next_a, passed_a, near_b, passed_b)
    came_next_a = swap_with(joint_a, "shard", 2)
    came_near_b = swap_with(joint_b, "shard", 1)
    return [[came_near_a, came_next_a], [came_near_b, came_next_b]]


def add_pairs(*refs):
    for j, out_ref in enumerate(refs[2 * (len(refs) // 3) :]):
        total = refs[2 * j][...].astype(f32) + refs[2 * j + 1][...].astype(f32)
        out_ref[...] = total.astype(out_ref.dtype)


def spread_rows(own):
    count = lax.axis_size("ctx")
    mine = [own]
    for k in range(1, count):
        if k == 1 or k % 2 == 0:
            mine.append(swap_with(own, "ctx", k))
        else:
            mine.append(swap_with(mine[k - 1], "ctx", 1))
    return mine + [swap_with(piece, "tp", 1) for piece in mine]


def in_vmem(body, outs, *operands, scratch=(), flops=0, mib=16):
    shapes = [jax.ShapeDtypeStruct(shape, dtype) for shape, dtype in outs]
    moved = sum(x.size * x.dtype.itemsize for x in (*operands, *shapes))
    return pl.pallas_call(
        body,
        out_shape=shapes,
        in_specs=[pl.BlockSpec(memory_space=pltpu.VMEM)] * len(operands),
        out_specs=[pl.BlockSpec(memory_space=pltpu.VMEM)] * len(shapes),
        scratch_shapes=list(scratch),
        compiler_params=pltpu.CompilerParams(vmem_limit_bytes=mib << 20),
        cost_estimate=pl.CostEstimate(flops=flops, bytes_accessed=moved, transcendentals=0),
    )(*operands)


def by_rows(rows, weight):
    return lax.dot_general(rows, weight, (((1,), (1,)), ((), ())), preferred_element_type=f32)


def down_rows(left, right):
    return lax.dot_general(left, right, (((0,), (0,)), ((), ())), preferred_element_type=f32)


def block_start(step, core, rows):
    return pl.multiple_of((2 * jnp.bitwise_xor(lax.axis_index("ctx"), step) + core) * rows, rows)


def delayed(values, steps):
    length = values.shape[0]
    rolled = pltpu.roll(values, steps % length, 0)
    row = lax.broadcasted_iota(jnp.int32, values.shape, 0)
    kept = row >= steps if steps > 0 else row < length + steps
    return jnp.where(kept, rolled, 0.0)


def convolved(b_part, x_part, taps):
    product = b_part * x_part
    one, two = delayed(product, 1), delayed(product, 2)
    return product, one, two, taps[0:1] * two + taps[1:2] * one + taps[2:3] * product


def own_columns(groups, block, shape):
    row = lax.broadcasted_iota(jnp.int32, shape, 0)
    ahead = lax.broadcasted_iota(jnp.int32, shape, 1) - row
    stride = shape[1] // groups
    found = jnp.zeros(shape, f32)
    group_at = lax.axis_index("shard")
    within = lax.axis_index("ctx") * lax.axis_size("tp") + lax.axis_index("tp")
    for k in range(groups):
        base = jnp.bitwise_xor(group_at, k) * stride + (within - k) * block
        inside = (row >= k * block) & (row < (k + 1) * block)
        found = jnp.where(inside & (ahead == base), 1.0, found)
    return found


def mixer_forward(count, groups, *refs):
    pieces, parts = refs[: 2 * count], refs[2 * count : 2 * count + groups]
    gain_ref, conv_ref, h_ref, w_ref, p_ref, y_ref, taps_ref, keep_ref, send_ref = refs[
        2 * count + groups :
    ]
    rows = pieces[0].shape[0]
    block, channels = parts[0].shape[1], y_ref.shape[1]
    core = lax.axis_index("tp")
    taps_ref[...] = lax.dot_general(
        conv_ref[...],
        own_columns(groups, block, (channels, conv_ref.shape[1])),
        (((1,), (1,)), ((), ())),
        precision=lax.Precision.HIGHEST,
        preferred_element_type=f32,
    )
    for k in range(4):
        for s in range(groups):
            w_ref[k * channels + s * block : k * channels + (s + 1) * block, :] = parts[s][k]
    gain = gain_ref[0:1, :]
    for j in range(2 * count):
        x = pieces[j][...].astype(f32)
        scale = lax.rsqrt(jnp.mean(x * x, axis=-1, keepdims=True) + norm_eps)
        side = core if j < count else 1 - core
        h_ref[pl.ds(block_start(j % count, side, rows), rows), :] = (x * scale * gain).astype(bf16)
    p_ref[...] = by_rows(h_ref[...], w_ref[: 3 * channels, :])
    in_b, in_c = p_ref[:, :channels], p_ref[:, channels : 2 * channels]
    in_x = p_ref[:, 2 * channels :]
    mixed = convolved(in_b, in_x, taps_ref[...])[3]
    y_ref[...] = (in_c * mixed).astype(bf16)
    out_w = w_ref[3 * channels :, :]
    for side, out_ref in ((1 - core, send_ref), (core, keep_ref)):
        starts = [block_start(k, side, rows) for k in range(count)]
        rows_of = [y_ref[pl.ds(at, rows), :] for at in starts]
        part = jnp.dot(jnp.concatenate(rows_of, axis=0), out_w, preferred_element_type=f32)
        out_ref[...] = part.astype(out_ref.dtype)


def halves_of(values):
    coarse = values.astype(bf16)
    return coarse, (values - coarse.astype(f32)).astype(bf16)


def whole_of(ref, at):
    rows = small_rows
    return ref[at : at + rows, :].astype(f32) + ref[at + rows : at + 2 * rows, :].astype(f32)


def mixer_backward(count, groups, *refs):
    pieces = refs[: 2 * count]
    h_ref, w_ref, p_ref, gain_ref, taps_ref, gain_two_ref = refs[2 * count : 2 * count + 6]
    dm_ref, dp_ref, keep_ref, send_ref, small_ref = refs[2 * count + 6 :]
    rows, side_rows = pieces[0].shape[0], count * pieces[0].shape[0]
    channels = taps_ref.shape[1]
    core = lax.axis_index("tp")
    for j in range(2 * count):
        side = core if j < count else 1 - core
        dm_ref[pl.ds(block_start(j % count, side, rows), rows), :] = pieces[j][...]
    grad_gated = by_rows(dm_ref[...], w_ref[3 * channels :, :])
    in_b, in_c = p_ref[:, :channels], p_ref[:, channels : 2 * channels]
    in_x = p_ref[:, 2 * channels :]
    taps = taps_ref[...]
    product, one, two, mixed = convolved(in_b, in_x, taps)
    grad_mixed = grad_gated * in_c
    next_one, next_two = delayed(grad_mixed, -1), delayed(grad_mixed, -2)
    grad_prod = taps[0:1] * next_two + taps[1:2] * next_one + taps[2:3] * grad_mixed
    dp_ref[:, :channels] = (grad_prod * in_x).astype(bf16)
    dp_ref[:, channels : 2 * channels] = (grad_gated * mixed).astype(bf16)
    dp_ref[:, 2 * channels :] = (grad_prod * in_b).astype(bf16)
    tap_sums = [
        jnp.sum(grad_mixed * shifted, axis=0, keepdims=True) for shifted in (two, one, product)
    ]
    small_ref[...] = jnp.zeros(small_ref.shape, f32)
    small_ref[2:5, :] = jnp.dot(
        jnp.concatenate(tap_sums, axis=0),
        own_columns(groups, channels // groups, (channels, h_ref.shape[1])),
        precision=lax.Precision.HIGHEST,
        preferred_element_type=f32,
    )
    small_ref[1:2, :] = gain_two_ref[...]
    gain_sum = jnp.zeros((1, gain_ref.shape[1]), f32)
    for side, out_ref in ((1 - core, send_ref), (core, keep_ref)):
        starts = [block_start(k, side, rows) for k in range(count)]
        grads = jnp.concatenate([dp_ref[pl.ds(at, rows), :] for at in starts], axis=0)
        part = jnp.dot(grads, w_ref[: 3 * channels, :], preferred_element_type=f32)
        out_ref[:side_rows, :] = part.astype(out_ref.dtype)
        normed = jnp.concatenate([h_ref[pl.ds(at, rows), :] for at in starts], axis=0)
        gain_sum = gain_sum + jnp.sum(part * normed.astype(f32), axis=0, keepdims=True)
    small_ref[0:1, :] = gain_sum / gain_ref[0:1, :]
    coarse, fine = halves_of(small_ref[...])
    send_ref[side_rows:, :] = jnp.concatenate([coarse, fine], axis=0)
    keep_ref[side_rows:, :] = coarse.astype(f32) + fine.astype(f32)


def mixer_weight_grads(groups, dp_ref, h_ref, y_ref, dm_ref, *outs):
    block = outs[0].shape[1]
    channels = y_ref.shape[1]
    inner = down_rows(dp_ref[...], h_ref[...])
    outer = down_rows(y_ref[...], dm_ref[...])
    for s in range(groups):
        for k in range(3):
            at = k * channels + s * block
            outs[s][k] = inner[at : at + block].astype(outs[s].dtype)
        outs[s][3] = outer[s * block : (s + 1) * block].astype(outs[s].dtype)


def ffn_gather(count, *refs):
    *pieces, g_ref, w_ref, down_ref = refs
    g_pieces, parts = pieces[: 2 * count], pieces[2 * count :]
    rows, hidden = g_pieces[0].shape[0], down_ref.shape[0]
    for j in range(2 * count):
        g_ref[j * rows : (j + 1) * rows, :] = g_pieces[j][...]
    block, columns = parts[0].shape[1:]
    for j, part in enumerate(parts):
        at, side = (j // 2) * block, slice((j % 2) * columns, (j % 2 + 1) * columns)
        w_ref[at : at + block, side] = part[0]
        w_ref[hidden + at : hidden + at + block, side] = part[1]
        down_ref[at : at + block, side] = part[2]


def ffn_rows(count, first, *refs):
    pieces = refs[:count]
    g_ref, w_ref, down_ref, h_ref, act_ref, gate_ref, up_ref, part_ref = refs[count:]
    rows, hidden = pieces[0].shape[0], down_ref.shape[0]
    for j in range(count):
        h_ref[j * rows : (j + 1) * rows, :] = pieces[j][...]
    gate = by_rows(h_ref[...], w_ref[:hidden, :])
    up = by_rows(h_ref[...], w_ref[hidden:, :])
    sigmoid = jax.nn.sigmoid(gate)
    gate_act = gate * sigmoid
    act_ref[...] = (gate_act * up).astype(bf16)
    grad_act = by_rows(g_ref[first : first + count * rows, :], down_ref[...])
    up_ref[...] = (grad_act * gate_act).astype(bf16)
    gate_ref[...] = (grad_act * up * sigmoid * (1.0 + gate * (1.0 - sigmoid))).astype(bf16)
    part = jnp.dot(gate_ref[...], w_ref[:hidden, :], preferred_element_type=f32)
    part = part + jnp.dot(up_ref[...], w_ref[hidden:, :], preferred_element_type=f32)
    part_ref[...] = part.astype(part_ref.dtype)


def ffn_down(mine_ref, other_ref, down_ref, keep_ref, send_ref):
    for act_ref, out_ref in ((other_ref, send_ref), (mine_ref, keep_ref)):
        part = jnp.dot(act_ref[...], down_ref[...], preferred_element_type=f32)
        out_ref[...] = part.astype(out_ref.dtype)


def ffn_weight_grads(*refs):
    mine, other = refs[:4], refs[4:8]
    g_ref, own_ref, *halves = refs[8:]
    block, columns = own_ref.shape[1], halves[0].shape[2]
    count = mine[0].shape[0]
    for k, at in enumerate((2, 3, 1)):
        rights = (g_ref[:count, :], g_ref[count:, :]) if at == 1 else (mine[0][...], other[0][...])
        term = down_rows(mine[at][...], rights[0]) + down_rows(other[at][...], rights[1])
        own_ref[k] = term[:block]
        for j, out_ref in enumerate(halves):
            row, side = (1 + j // 2) * block, (j % 2) * columns
            out_ref[k] = term[row : row + block, side : side + columns].astype(bf16)


def ffn_adam(half_parts, *refs):
    own_ref, parts = refs[0], refs[1 : 1 + 2 * half_parts]
    weight, first, second, grad_out, *outs = refs[1 + 2 * half_parts :]
    columns = parts[0].shape[2]
    for k in range(3):
        for j in range(2):
            side = slice(j * columns, (j + 1) * columns)
            grad = own_ref[k, :, side]
            for part in parts[j * half_parts : (j + 1) * half_parts]:
                grad = grad + part[k].astype(f32)
            grad_out[k, :, side] = grad
            news = adam_update(
                weight[k, :, side],
                grad,
                first[k, :, side],
                second[k, :, side],
                matrix_rate,
                decay_rate,
            )
            for out, new in zip(outs, news):
                out[k, :, side] = new


def mixer_adam(groups, *refs):
    own_ref, *parts = refs[:groups]
    weight, first, second, grad_out, weight_out, first_out, second_out = refs[groups:]
    for k in range(4):
        grad = own_ref[k]
        for part in parts:
            grad = grad + part[k].astype(f32)
        news = adam_update(
            weight[:, k, :], grad, first[:, k, :], second[:, k, :], matrix_rate, decay_rate
        )
        grad_out[:, k, :] = grad
        for out, new in zip((weight_out, first_out, second_out), news):
            out[:, k, :] = new


def pair_kernel(kept_ref, got_ref, *outs):
    rows = outs[0].shape[0]
    for k, out_ref in enumerate(outs):
        at = slice(k * rows, (k + 1) * rows)
        out_ref[...] = (kept_ref[at, :] + got_ref[at, :].astype(f32)).astype(out_ref.dtype)


def pair_with_small(kept_ref, got_ref, *outs):
    rows = outs[0].shape[0] - small_rows
    count = len(outs)
    small = kept_ref[count * rows :, :] + whole_of(got_ref, count * rows)
    rounded = small.astype(bf16)
    for k, out_ref in enumerate(outs):
        at = slice(k * rows, (k + 1) * rows)
        pair = kept_ref[at, :] + got_ref[at, :].astype(f32)
        out_ref[:rows, :] = pair.astype(out_ref.dtype)
        out_ref[rows:, :] = rounded.astype(out_ref.dtype)


def total_of(own_ref, got_refs, rows=None):
    total = own_ref[:rows, :]
    for got in got_refs:
        total = total + got[:rows, :].astype(f32)
    return total


def own_rows(rows_ref, out_ref):
    count = out_ref.shape[0]
    start = pl.multiple_of(lax.axis_index("tp") * count, count)
    out_ref[...] = rows_ref[0, pl.ds(start, count), :]


def join_rows(mine_ref, other_ref, out_ref):
    count, core = mine_ref.shape[0], lax.axis_index("tp")
    out_ref[0, pl.ds(pl.multiple_of(core * count, count), count), :] = mine_ref[...]
    out_ref[0, pl.ds(pl.multiple_of((1 - core) * count, count), count), :] = other_ref[...]


def prepare_ffn(weight_ref, *outs):
    columns = outs[0].shape[2]
    for j, out_ref in enumerate(outs):
        out_ref[...] = weight_ref[:, :, j * columns : (j + 1) * columns].astype(bf16)


def prepare_mixer(weight_ref, out_ref):
    for k in range(4):
        out_ref[k] = weight_ref[:, k, :].astype(bf16)


def second_norm(*refs):
    own_ref, *got = refs[:-5]
    x_ref, gain_ref, resid_ref, normed_ref, h_ref = refs[-5:]
    residual = x_ref[...].astype(f32) + total_of(own_ref, got)
    resid_ref[...] = residual
    normed = residual * lax.rsqrt(jnp.mean(residual * residual, axis=-1, keepdims=True) + norm_eps)
    normed_ref[...] = normed
    h_ref[...] = (normed * gain_ref[1:2, :]).astype(bf16)


def second_norm_backward(*refs):
    own_ref, *got = refs[:-7]
    resid_ref, normed_ref, g_ref, gain_ref, grad_ref, dm_ref, gain_part_ref = refs[-7:]
    grad_h = total_of(own_ref, got)
    normed, residual = normed_ref[...], resid_ref[...]
    scale = lax.rsqrt(jnp.mean(residual * residual, axis=-1, keepdims=True) + norm_eps)
    grad = g_ref[...].astype(f32) + norm_backward(grad_h * gain_ref[1:2, :], normed, scale)
    grad_ref[...] = grad
    dm_ref[...] = grad.astype(bf16)
    gain_part_ref[...] = jnp.sum(grad_h * normed, axis=0, keepdims=True)


def first_norm_backward(*refs):
    own_ref, *got = refs[:-5]
    x_ref, grad_ref, gain_ref, out_ref, small_ref = refs[-5:]
    rows = x_ref.shape[0]
    x = x_ref[...].astype(f32)
    scale = lax.rsqrt(jnp.mean(x * x, axis=-1, keepdims=True) + norm_eps)
    out_ref[...] = grad_ref[...] + norm_backward(
        total_of(own_ref, got, rows) * gain_ref[0:1, :], x * scale, scale
    )
    small_ref[...] = tree_sum([ref[rows:, :].astype(f32) for ref in (own_ref, *got)])


def small_adam(groups, *refs):
    pieces, operands, outs = refs[:groups], refs[groups : groups + 6], refs[groups + 6 :]
    total = tree_sum([piece[...] for piece in pieces])
    for which, grad in enumerate((total[0:2], total[2:5])):
        weight, first, second = (ref[...] for ref in operands[3 * which : 3 * which + 3])
        news = adam_update(weight, grad, first, second, small_rate, 0.0)
        for out, value in zip(outs[4 * which : 4 * which + 4], (grad, *news)):
            out[...] = value


def output_kernel(*refs):
    own_ref, *got = refs[:-2]
    resid_ref, out_ref = refs[-2:]
    out_ref[...] = (resid_ref[...] + total_of(own_ref, got)).astype(out_ref.dtype)


def collect_rows(kept, sent, small=False, passed=False):
    count = lax.axis_size("ctx")
    width = kept.shape[1]
    rows = (kept.shape[0] - small_rows * small) // count
    outs = [((rows + small_rows * small, width), f32)]
    outs += [((rows + small_rows * small, width), bf16)] * (count - 1)
    got = swap_with(sent, "tp", 1)
    pieces = in_vmem(pair_with_small if small else pair_kernel, outs, kept, got)
    if not passed or count != 4:
        return [pieces[0]] + [swap_with(pieces[k], "ctx", k) for k in range(1, count)]
    came = swap_with(pieces[3], "ctx", 1)
    near = swap_with(pieces[1], "ctx", 1)
    joint = in_vmem(add_pairs, outs[2:3], pieces[2], came)
    return [pieces[0], near, swap_with(joint[0], "ctx", 2)]


def per_device(
    inputs,
    cotangent,
    mixer_matrix,
    ffn_weight,
    conv_weight,
    norm_gains,
    mixer_first,
    mixer_second,
    ffn_first,
    ffn_second,
    conv_first,
    conv_second,
    gain_first,
    gain_second,
):
    shard_count = lax.axis_size("shard")
    ctx_count = lax.axis_size("ctx")
    tp_count = lax.axis_size("tp")
    seq_count, tok_count, width = inputs.shape
    assert seq_count == 1 and tp_count == 2
    half = tok_count // tp_count
    seq_len = tok_count * ctx_count

    half_shape, half_sent = ((half, width), f32), ((half, width), bf16)

    def both_halves(mine):
        other = swap_with(mine, "tp", 1)
        whole = ((1, tok_count, width), mine.dtype)
        return in_vmem(join_rows, [whole], mine, other)[0]

    x_half = in_vmem(own_rows, [half_sent], inputs)[0]
    x_pieces = spread_rows(x_half)
    block = mixer_matrix.shape[0]
    mixer_own = in_vmem(prepare_mixer, [((4, block, width), bf16)], mixer_matrix)[0]
    mixer_parts = [mixer_own] + [swap_with(mixer_own, "shard", k) for k in range(1, shard_count)]
    ffn_block = ffn_weight.shape[0]
    ffn_own = in_vmem(
        prepare_ffn, [((3, ffn_block, width // 2), bf16)] * 2, ffn_weight.transpose(1, 0, 2)
    )
    ffn_halves = across_shard(ffn_own)
    ffn_parts = [half for halves in ffn_halves for half in halves]
    g_half = in_vmem(own_rows, [half_sent], cotangent)[0]
    g_pieces = spread_rows(g_half)

    channels, hidden = block * shard_count, ffn_block * shard_count
    mine_count = seq_len // 2
    parted = [((mine_count, width), f32), ((mine_count, width), bf16)]

    h_one, mixer_w, projected, gated, taps, kept, sent = in_vmem(
        functools.partial(mixer_forward, ctx_count, shard_count),
        [
            ((seq_len, width), bf16),
            ((4 * channels, width), bf16),
            ((seq_len, 3 * channels), f32),
            ((seq_len, channels), bf16),
            ((3, channels), f32),
        ]
        + parted,
        *x_pieces,
        *mixer_parts,
        norm_gains,
        conv_weight,
        flops=8 * seq_len * channels * width,
    )
    residual, normed_two, h_two_own = in_vmem(
        second_norm,
        [half_shape, half_shape, half_sent],
        *collect_rows(kept, sent),
        x_half,
        norm_gains,
    )

    hidden_rows = ((mine_count, hidden), bf16)
    g_all, gate_up_w, down_w = in_vmem(
        functools.partial(ffn_gather, ctx_count),
        [
            ((seq_len, width), bf16),
            ((2 * hidden, width), bf16),
            ((hidden, width), bf16),
        ],
        *g_pieces,
        *ffn_parts,
    )
    h_pieces = spread_rows(h_two_own)
    sides = []
    for j in range(2):
        sides.append(
            in_vmem(
                functools.partial(ffn_rows, ctx_count, j * mine_count),
                [((mine_count, width), bf16), hidden_rows, hidden_rows, hidden_rows, parted[j]],
                *h_pieces[j * ctx_count : (j + 1) * ctx_count],
                g_all,
                gate_up_w,
                down_w,
                flops=5 * seq_len * hidden * width,
            )
        )
    (*mine, kept), (*other, sent) = sides
    grad_resid, grad_mix_own, gain_two_part = in_vmem(
        second_norm_backward,
        [half_shape, half_sent, ((1, width), f32)],
        *collect_rows(kept, sent),
        residual,
        normed_two,
        g_half,
        norm_gains,
    )
    kept, sent = in_vmem(
        ffn_down, parted, mine[1], other[1], down_w, flops=2 * seq_len * hidden * width
    )
    ffn_pieces = collect_rows(kept, sent, passed=True)
    ffn_terms = in_vmem(
        ffn_weight_grads,
        [((3, ffn_block, width), f32)]
        + [((3, ffn_block, width // 2), bf16)] * (2 * (shard_count - 1)),
        *mine,
        *other,
        g_all,
        flops=6 * seq_len * hidden * width,
    )
    ffn_got = owners_terms(list(zip(ffn_terms[1::2], ffn_terms[2::2])))

    grad_mix_all, grad_triple, kept, sent = in_vmem(
        functools.partial(mixer_backward, ctx_count, shard_count),
        [
            ((seq_len, width), bf16),
            ((seq_len, 3 * channels), bf16),
            ((mine_count + small_rows, width), f32),
            ((mine_count + 2 * small_rows, width), bf16),
        ],
        *spread_rows(grad_mix_own),
        h_one,
        mixer_w,
        projected,
        norm_gains,
        taps,
        gain_two_part,
        scratch=[pltpu.VMEM((small_rows, width), f32)],
        flops=8 * seq_len * channels * width,
    )
    in_pieces = collect_rows(kept, sent, small=True)
    mixer_terms = in_vmem(
        functools.partial(mixer_weight_grads, shard_count),
        [((4, block, width), f32)] + [((4, block, width), bf16)] * (shard_count - 1),
        grad_triple,
        h_one,
        gated,
        grad_mix_all,
        flops=8 * seq_len * channels * width,
    )
    mixer_got = [swap_with(mixer_terms[k], "shard", k) for k in range(1, shard_count)]
    ffn_news = in_vmem(
        functools.partial(ffn_adam, len(ffn_got[0])),
        [((3, ffn_block, width), f32)] * 4,
        ffn_terms[0],
        *ffn_got[0],
        *ffn_got[1],
        *(value.transpose(1, 0, 2) for value in (ffn_weight, ffn_first, ffn_second)),
    )
    ffn_grad, ffn_new, ffn_first_new, ffn_second_new = (
        value.transpose(1, 0, 2) for value in ffn_news
    )
    out_own = in_vmem(output_kernel, [half_sent], *ffn_pieces, residual)[0]
    output = both_halves(out_own)
    input_grad, small = in_vmem(
        first_norm_backward,
        [half_shape, ((small_rows, width), f32)],
        *in_pieces,
        x_half,
        grad_resid,
        norm_gains,
    )
    input_grad = both_halves(input_grad)
    (
        gain_grad,
        gain_new,
        gain_first_new,
        gain_second_new,
        conv_grad,
        conv_new,
        conv_first_new,
        conv_second_new,
    ) = in_vmem(
        functools.partial(small_adam, shard_count),
        [(norm_gains.shape, f32)] * 4 + [(conv_weight.shape, f32)] * 4,
        small,
        *(swap_with(small, "shard", k) for k in range(1, shard_count)),
        norm_gains,
        gain_first,
        gain_second,
        conv_weight,
        conv_first,
        conv_second,
    )
    mixer_grad, mixer_new, mixer_first_new, mixer_second_new = in_vmem(
        functools.partial(mixer_adam, shard_count),
        [(mixer_matrix.shape, f32)] * 4,
        mixer_terms[0],
        *mixer_got,
        mixer_matrix,
        mixer_first,
        mixer_second,
    )
    return (
        output,
        input_grad,
        mixer_grad,
        ffn_grad,
        conv_grad,
        gain_grad,
        mixer_new,
        ffn_new,
        conv_new,
        gain_new,
        mixer_first_new,
        mixer_second_new,
        ffn_first_new,
        ffn_second_new,
        conv_first_new,
        conv_second_new,
        gain_first_new,
        gain_second_new,
    )


def solution(mesh):
    tokens = P("shard", "ctx", None)
    rows = P(("shard", "ctx", "tp"), None, None)
    in_specs = (tokens, tokens, rows, rows, P(), P(), rows, rows, rows, rows, P(), P(), P(), P())
    out_specs = (
        (tokens, tokens, rows, rows, P(), P(), rows, rows, P(), P())
        + (rows, rows, rows, rows)
        + (P(), P(), P(), P())
    )

    return jax.shard_map(
        per_device, mesh=mesh, in_specs=in_specs, out_specs=out_specs, check_vma=False
    )
```
